256 devices in a mesh: gx: 32 (over z_lo, x, core), gy: 8 (over z_hi, y).
Axes of the slice: x: 4, y: 4, z: 8 (z_hi: 2, z_lo: 4; z = z_hi * 4 + z_lo), core: 2. Of those that a mesh axis runs over, the one named last changes fastest.
Arguments:
- right_side: float32 [512, 1024, 128], P('gx', 'gy'), may hold values from -50 to 50
- conductivity: float32 [512, 1024, 128], P('gx', 'gy'), may hold values from 0.2 to 5
Outputs:
- solution_field: float32 [512, 1024, 128], P('gx', 'gy')
- residual: float32 [512, 1024, 128], P('gx', 'gy')
The draws below stay inside these ranges and needn't reach their ends.
All inputs are finite; a program needn't handle non-finite values.
Results may differ from the reference program's by a relative error of at most 0.0085.
Values sent between devices are 32-bit elements; how exact they have to be, the bound alone decides.
A program may use at most 64 MiB of HBM per device.

```python
import math
import jax
import jax.numpy as jnp
from jax import lax

CX = 16
CY = 128
MARGIN = 4
SWEEPS = 3
ITERS = 2
NX = 512
NY = 1024
NZ = 128
N_GX = 32
N_GY = 8


def draw_right_side(key, part):
    ramp_x = 3.0 ** (jnp.arange(NX, dtype=jnp.float32) / NX)
    ramp_y = 1.5 ** (jnp.arange(NY, dtype=jnp.float32) / NY)
    scale = ramp_x[:, None, None] * ramp_y[None, :, None]
    base = jnp.clip(jax.random.normal(key, (NX, NY, NZ), jnp.float32), -6.0, 6.0)
    return (base * scale).astype(jnp.float32)


def level_of(stream_key, shape, shards, least, high):
    factor_of = 1.0
    for axis_at, shards_of in shards:
        steps = jax.random.uniform(jax.random.fold_in(jax.random.fold_in(stream_key, 6), axis_at), (shards_of,), jnp.float32, least / len(shards), high / len(shards))
        factor_of = factor_of * jnp.repeat(jnp.exp(steps), shape[axis_at] // shards_of).reshape((-1,) + (1,) * (len(shape) - 1 - axis_at))
    return factor_of


def setup_inputs(seed: int = 0) -> dict:
    key_list = jax.random.split(jax.random.key(seed), 3)
    return {
        "right_side": draw_right_side(jax.random.fold_in(key_list[2], 71), 0),
        "conductivity": jnp.clip(jnp.exp(math.log(5.0) - 3.218876 * jax.random.uniform(key_list[1], (NX, NY, NZ), jnp.float32) ** level_of(key_list[1], (NX, NY, NZ), ((0, 32), (1, 8)), -0.2, 0.2)), 0.2, 5.0),
    }


absorb = 0.05
theta = 1.05
delta = 0.95


def coefficients(wide):
    padded = jnp.pad(wide, ((0, 0), (0, 0), (1, 1)))
    center = padded[1:-1, 1:-1, 1:-1]
    diagonal = absorb + jnp.zeros_like(center)
    for beside in (padded[:-2, 1:-1, 1:-1], padded[2:, 1:-1, 1:-1], padded[1:-1, :-2, 1:-1],
                   padded[1:-1, 2:, 1:-1], padded[1:-1, 1:-1, :-2], padded[1:-1, 1:-1, 2:]):
        diagonal = diagonal + jnp.where(beside > 0, 0.5 * (center + beside), center)
    living = center > 0
    face_x = jnp.where(living[1:] & living[:-1], 0.5 * (center[1:] + center[:-1]), 0.0)
    face_y = jnp.where(living[:, 1:] & living[:, :-1], 0.5 * (center[:, 1:] + center[:, :-1]), 0.0)
    face_z = jnp.where(living[:, :, 1:] & living[:, :, :-1], 0.5 * (center[:, :, 1:] + center[:, :, :-1]), 0.0)
    return diagonal, face_x, face_y, face_z


def local_apply(field, coeffs):
    diagonal, face_x, face_y, face_z = coeffs
    beside = jnp.pad(face_x * field[1:], ((0, 1), (0, 0), (0, 0))) + jnp.pad(face_x * field[:-1], ((1, 0), (0, 0), (0, 0)))
    beside = beside + jnp.pad(face_y * field[:, 1:], ((0, 0), (0, 1), (0, 0))) + jnp.pad(face_y * field[:, :-1], ((0, 0), (1, 0), (0, 0)))
    beside = beside + jnp.pad(face_z * field[:, :, 1:], ((0, 0), (0, 0), (0, 1))) + jnp.pad(face_z * field[:, :, :-1], ((0, 0), (0, 0), (1, 0)))
    return diagonal * field - beside


def chebyshev(source, coeffs):
    inverse = 1.0 / coeffs[0]
    ratio_sig = theta / delta
    ratio_now = 1.0 / ratio_sig
    update = inverse * source / theta
    answer = update
    for sweep in range(SWEEPS - 1):
        ratio_new = 1.0 / (2.0 * ratio_sig - ratio_now)
        update = (ratio_new * ratio_now) * update + (2.0 * ratio_new / delta) * inverse * (source - local_apply(answer, coeffs))
        answer = answer + update
        ratio_now = ratio_new
    return answer


def precondition(residue, kappa_wide):
    padded = jnp.pad(residue, ((MARGIN, MARGIN), (MARGIN, MARGIN), (0, 0)))
    naught = jnp.zeros((), jnp.int32)

    def one_block(total, block):
        start_x = (block // N_GY) * CX
        start_y = (block % N_GY) * CY
        kappa = lax.dynamic_slice(kappa_wide, (start_x, start_y, naught), (CX + 2 * MARGIN + 2, CY + 2 * MARGIN + 2, NZ))
        source = lax.dynamic_slice(padded, (start_x, start_y, naught), (CX + 2 * MARGIN, CY + 2 * MARGIN, NZ))
        local = chebyshev(source, coefficients(kappa))
        current = lax.dynamic_slice(total, (start_x, start_y, naught), local.shape)
        return lax.dynamic_update_slice(total, current + local, (start_x, start_y, naught)), None

    total, unused = lax.scan(one_block, jnp.zeros_like(padded), jnp.arange(N_GX * N_GY, dtype=jnp.int32))
    return total[MARGIN:-MARGIN, MARGIN:-MARGIN]


def reference(right_side, conductivity):
    kappa_wide = jnp.pad(conductivity, ((MARGIN + 1, MARGIN + 1), (MARGIN + 1, MARGIN + 1), (0, 0)))
    whole = coefficients(jnp.pad(conductivity, ((1, 1), (1, 1), (0, 0))))
    solution_field = jnp.zeros_like(right_side)
    residual = right_side
    precond = precondition(residual, kappa_wide)
    direction = precond
    dot_now = jnp.sum(residual * precond)
    for step in range(ITERS):
        image = local_apply(direction, whole)
        step_size = dot_now / jnp.sum(direction * image)
        solution_field = solution_field + step_size * direction
        residual = residual - step_size * image
        if step + 1 < ITERS:
            precond = precondition(residual, kappa_wide)
            dot_next = jnp.sum(residual * precond)
            direction = precond + (dot_next / dot_now) * direction
            dot_now = dot_next
    return solution_field, residual
```

```python
import jax
import jax.numpy as jnp
from jax import lax
from jax.sharding import PartitionSpec as P

MARGIN = 4
SWEEPS = 3
ITERS = 2


absorb = 0.05
theta = 1.05
delta = 0.95


def with_halo(block, sides, width):
    for axis, dim in sides:
        count = lax.axis_size(axis)
        forward = [(i, i + 1) for i in range(count - 1)]
        backward = [(target, source) for source, target in forward]
        low = lax.ppermute(
            lax.slice_in_dim(block, block.shape[dim] - width, None, axis=dim), axis, forward
        )
        high = lax.ppermute(lax.slice_in_dim(block, 0, width, axis=dim), axis, backward)
        block = jnp.concatenate([low, block, high], axis=dim)
    return block


def from_behind(x, axis, by):
    size = lax.axis_size(axis)
    pairs = [(i, i + by) for i in range(size) if 0 <= i + by < size]
    return lax.ppermute(x, axis, pairs)


def coefficients(wide):
    padded = jnp.pad(wide, ((0, 0), (0, 0), (1, 1)))
    center = padded[1:-1, 1:-1, 1:-1]
    diagonal = absorb + jnp.zeros_like(center)
    for beside in (
        padded[:-2, 1:-1, 1:-1],
        padded[2:, 1:-1, 1:-1],
        padded[1:-1, :-2, 1:-1],
        padded[1:-1, 2:, 1:-1],
        padded[1:-1, 1:-1, :-2],
        padded[1:-1, 1:-1, 2:],
    ):
        diagonal = diagonal + jnp.where(beside > 0, 0.5 * (center + beside), center)
    living = center > 0
    face_x = jnp.where(living[1:] & living[:-1], 0.5 * (center[1:] + center[:-1]), 0.0)
    face_y = jnp.where(living[:, 1:] & living[:, :-1], 0.5 * (center[:, 1:] + center[:, :-1]), 0.0)
    face_z = jnp.where(
        living[:, :, 1:] & living[:, :, :-1], 0.5 * (center[:, :, 1:] + center[:, :, :-1]), 0.0
    )
    return (diagonal, face_x, face_y, face_z)


def local_apply(field, coeffs):
    diagonal, face_x, face_y, face_z = coeffs
    beside = jnp.pad(face_x * field[1:], ((0, 1), (0, 0), (0, 0))) + jnp.pad(
        face_x * field[:-1], ((1, 0), (0, 0), (0, 0))
    )
    beside = (
        beside
        + jnp.pad(face_y * field[:, 1:], ((0, 0), (0, 1), (0, 0)))
        + jnp.pad(face_y * field[:, :-1], ((0, 0), (1, 0), (0, 0)))
    )
    beside = (
        beside
        + jnp.pad(face_z * field[:, :, 1:], ((0, 0), (0, 0), (0, 1)))
        + jnp.pad(face_z * field[:, :, :-1], ((0, 0), (0, 0), (1, 0)))
    )
    return diagonal * field - beside


def chebyshev(source, coeffs):
    inverse = 1.0 / coeffs[0]
    ratio_sig = theta / delta
    ratio_now = 1.0 / ratio_sig
    update = inverse * source / theta
    answer = update
    for sweep in range(SWEEPS - 1):
        ratio_new = 1.0 / (2.0 * ratio_sig - ratio_now)
        update = ratio_new * ratio_now * update + 2.0 * ratio_new / delta * inverse * (
            source - local_apply(answer, coeffs)
        )
        answer = answer + update
        ratio_now = ratio_new
    return answer


def operate_brick(field, coeffs):
    width = field.shape[0]
    depth = field.shape[1]
    with_rim = with_halo(field, (("gx", 0), ("gy", 1)), 1)
    diagonal, face_x, face_y, face_z = coeffs
    edge = MARGIN
    faces_x = face_x[edge - 1 : width + edge, edge : depth + edge]
    faces_y = face_y[edge : width + edge, edge - 1 : depth + edge]
    faces_z = face_z[edge : width + edge, edge : depth + edge]
    diag_brick = diagonal[edge : width + edge, edge : depth + edge]
    along_x = with_rim[:, 1:-1]
    beside = faces_x[1:] * along_x[2:] + faces_x[:-1] * along_x[:-2]
    along_y = with_rim[1:-1]
    beside = beside + faces_y[:, 1:] * along_y[:, 2:] + faces_y[:, :-1] * along_y[:, :-2]
    beside = (
        beside
        + jnp.pad(faces_z * field[:, :, 1:], ((0, 0), (0, 0), (0, 1)))
        + jnp.pad(faces_z * field[:, :, :-1], ((0, 0), (0, 0), (1, 0)))
    )
    return diag_brick * field - beside


def give_back(extended):
    edge = MARGIN
    size_x = extended.shape[0] - 2 * edge
    from_high = from_behind(extended[:edge], "gx", -1)
    from_low = from_behind(extended[size_x + edge :], "gx", 1)
    middle = (
        extended[edge : size_x + edge].at[:edge].add(from_low).at[size_x - edge :].add(from_high)
    )
    size_y = middle.shape[1] - 2 * edge
    from_high = from_behind(middle[:, :edge], "gy", -1)
    from_low = from_behind(middle[:, size_y + edge :], "gy", 1)
    return (
        middle[:, edge : size_y + edge]
        .at[:, :edge]
        .add(from_low)
        .at[:, size_y - edge :]
        .add(from_high)
    )


def shards(right_side, conductivity):
    wide = with_halo(conductivity, (("gx", 0), ("gy", 1)), MARGIN + 1)
    coeffs = coefficients(wide)

    def smooth(residue):
        padded = with_halo(residue, (("gx", 0), ("gy", 1)), MARGIN)
        return give_back(chebyshev(padded, coeffs))

    z0 = smooth(right_side)
    w0 = operate_brick(z0, coeffs)
    z1 = smooth(w0)
    w1 = operate_brick(z1, coeffs)
    pairs = ((right_side, z0), (z0, w0), (right_side, z1), (w0, z1), (z0, w1), (z1, w1))
    dots = lax.psum(jnp.stack([jnp.sum(a * b) for a, b in pairs]), ("gx", "gy"))
    rz, zw, rz1, wz1, zw1, z1w1 = [dots[i] for i in range(6)]
    first = rz / zw
    next_rz = rz - first * (rz1 + zw) + first * first * wz1
    grow = 1.0 + next_rz / rz
    curve = grow * grow * zw - grow * first * (zw1 + wz1) + first * first * z1w1
    second = next_rz / curve
    c0 = first + second * grow
    c1 = second * first
    return (c0 * z0 - c1 * z1, right_side - c0 * w0 + c1 * w1)


def solution(mesh):
    in_specs = (P("gx", "gy", None), P("gx", "gy", None))
    out_specs = (P("gx", "gy", None), P("gx", "gy", None))
    return jax.shard_map(shards, mesh=mesh, in_specs=in_specs, out_specs=out_specs, check_vma=False)
```

```python
import itertools

import jax
import jax.numpy as jnp
from jax import lax
from jax.experimental import pallas as pl
from jax.experimental.pallas import tpu as pltpu
from jax.sharding import PartitionSpec as P

MESH = pl.DeviceIdType.MESH
MARGIN = 4
absorb = 0.05
theta = 1.05
delta = 0.95

sig = theta / delta
rho0 = 1.0 / sig
rho1 = 1.0 / (2.0 * sig - rho0)
rho2 = 1.0 / (2.0 * sig - rho1)
c1, c2 = rho1 * rho0, 2.0 * rho1 / delta
c3, c4 = rho2 * rho1, 2.0 * rho2 / delta
A1 = 1.0 + c1 + c2 * (theta - 1.0)
B1 = 0.5 * c2
A2 = 1.0 + c3 - c4
A0 = c4 * theta - c3
B2 = 0.5 * c4

KW, RW = 7, 6
GUARD = 8
YO = 16
XO = KW

SIZES = dict(c=2, x=4, z=4, y=4, h=2)
STAGES = (("c",), ("x", "y"), ("z", "h"))
NEAR = tuple((dx, dy) for dx in (-1, 0, 1) for dy in (-1, 0, 1) if (dx, dy) != (0, 0))


def offsets(dims):
    return [o for o in itertools.product(*[range(SIZES[d]) for d in dims]) if any(o)]


N_SLOTS = sum(len(offsets(dims)) for dims in STAGES)


def partner(gx, gy, dims, off):
    me = dict(c=gx % 2, x=(gx // 2) % 4, z=gx // 8, y=gy % 4, h=gy // 4)
    for d, o in zip(dims, off):
        me[d] = (me[d] + o) % SIZES[d]
    return (me["z"] * 8 + me["x"] * 2 + me["c"], me["h"] * 4 + me["y"])


def kernel(
    r_hbm, k_hbm, sol_hbm, res_hbm,
    K, R, INV, DIAG, FX, FY, FZ, Y0, Y1, Y0B, Z0, Z1, W0, W1, part, slots,
    load_sem, out_sem, send_sem, recv_sem, ar_send, ar_recv,
):
    cx, cy, nz = r_hbm.shape
    n_gx, n_gy = lax.axis_size("gx"), lax.axis_size("gy")
    gx, gy = lax.axis_index("gx"), lax.axis_index("gy")
    n_tiles = cy // 8

    def here(dx, dy):
        return (gx + dx >= 0) & (gx + dx < n_gx) & (gy + dy >= 0) & (gy + dy < n_gy)

    barrier = pltpu.get_barrier_semaphore()
    count = 0
    for dx, dy in NEAR:
        count = count + here(dx, dy).astype(jnp.int32)

        @pl.when(here(dx, dy))
        def _():
            pl.semaphore_signal(barrier, inc=1, device_id=(gx + dx, gy + dy), device_id_type=MESH)

    for dims in STAGES:
        for off in offsets(dims):
            pl.semaphore_signal(
                barrier, inc=1, device_id=partner(gx, gy, dims, off), device_id_type=MESH
            )
            count = count + 1

    own = (pl.ds(XO, cx), pl.ds(YO, cy))
    loads = [
        pltpu.make_async_copy(k_hbm, K.at[own], load_sem.at[0]),
        pltpu.make_async_copy(r_hbm, R.at[own], load_sem.at[1]),
    ]
    for load in loads:
        load.start()
    pl.semaphore_wait(barrier, count)

    def halo_copies(k, dx, dy):
        out = []
        for n, (src, dst, width) in enumerate(((k_hbm, K, KW), (r_hbm, R, RW))):
            if dx > 0:
                sx, tx = pl.ds(cx - width, width), pl.ds(XO - width, width)
            elif dx < 0:
                sx, tx = pl.ds(0, width), pl.ds(XO + cx, width)
            else:
                sx, tx = pl.ds(0, cx), pl.ds(XO, cx)
            if dy > 0:
                sy, ty = pl.ds(cy - 8, 8), pl.ds(YO - 8, 8)
            elif dy < 0:
                sy, ty = pl.ds(0, 8), pl.ds(YO + cy, 8)
            else:
                sy, ty = pl.ds(0, cy), pl.ds(YO, cy)
            out.append(
                pltpu.make_async_remote_copy(
                    src.at[sx, sy], dst.at[tx, ty], send_sem.at[2 * k + n], recv_sem.at[2 * k + n],
                    device_id=(gx + dx, gy + dy), device_id_type=MESH,
                )
            )
        return out

    for k, (dx, dy) in enumerate(NEAR):

        @pl.when(here(dx, dy))
        def _():
            for copy in halo_copies(k, dx, dy):
                copy.start()

    rows = cy + 16
    flat = lambda n: jnp.zeros((n, nz), jnp.float32)

    @pl.when(gx == 0)
    def _():
        for x in range(XO):
            K[x, pl.ds(YO - 8, rows)] = flat(rows)
            R[x, pl.ds(YO - 8, rows)] = flat(rows)

    @pl.when(gx == n_gx - 1)
    def _():
        for x in range(XO + cx, XO + cx + KW):
            K[x, pl.ds(YO - 8, rows)] = flat(rows)
            R[x, pl.ds(YO - 8, rows)] = flat(rows)

    for load in loads:
        load.wait()
    for k, (dx, dy) in enumerate(NEAR):

        @pl.when(here(-dx, -dy))
        def _():
            for copy in halo_copies(k, dx, dy):
                copy.wait_recv()

    @pl.when(gx == 0)
    def _():
        K[XO - 1, pl.ds(YO - 8, rows)] = K[XO, pl.ds(YO - 8, rows)]

    @pl.when(gx == n_gx - 1)
    def _():
        K[XO + cx, pl.ds(YO - 8, rows)] = K[XO + cx - 1, pl.ds(YO - 8, rows)]

    n_layers = cx + 2 * KW

    @pl.when(gy == 0)
    def _():
        for x in range(n_layers):
            K[x, pl.ds(YO - 8, 8)] = jnp.broadcast_to(K[x, pl.ds(YO, 1)], (8, nz))
            R[x, pl.ds(YO - 8, 8)] = flat(8)

    @pl.when(gy == n_gy - 1)
    def _():
        for x in range(n_layers):
            K[x, pl.ds(YO + cy, 8)] = jnp.broadcast_to(K[x, pl.ds(YO + cy - 1, 1)], (8, nz))
            R[x, pl.ds(YO + cy, 8)] = flat(8)

    lane = lax.broadcasted_iota(jnp.int32, (8, nz), 1)
    sub = lax.broadcasted_iota(jnp.int32, (8, nz), 0)
    first_lane, last_lane = lane == 0, lane == nz - 1
    one = jnp.float32(1.0)
    m_lo = jnp.where(gx > 0, one, 0.0)
    m_hi = jnp.where(gx < n_gx - 1, one, 0.0)
    has_lo, has_hi = gy > 0, gy < n_gy - 1
    n_lo = jnp.where(has_lo, one, 0.0)
    n_hi = jnp.where(has_hi, one, 0.0)

    def at(ref, x, row):
        return ref[x + XO, pl.ds(row, 8), :]

    def put(ref, x, row, value):
        ref[x + XO, pl.ds(row, 8), :] = value

    def tile_row(t):
        return pl.multiple_of(YO - 8 + 8 * t, 8)

    def coefficients(t, carry):
        r0 = tile_row(t)
        low, mid = at(K, -RW - 1, r0), at(K, -RW, r0)
        for x in range(-RW, cx + RW):
            high = at(K, x + 1, r0)
            up, down = at(K, x, r0 + 1), at(K, x, r0 - 1)
            right = jnp.where(last_lane, mid, pltpu.roll(mid, nz - 1, 1))
            left = jnp.where(first_lane, mid, pltpu.roll(mid, 1, 1))
            diag = (absorb + 3.0 * mid) + 0.5 * ((low + high) + (up + down) + (left + right))
            inv = 1.0 / diag
            put(DIAG, x, r0, diag)
            put(INV, x, r0, inv)
            put(FX, x, r0, mid + high)
            put(FY, x, r0, mid + up)
            put(FZ, x, r0, jnp.where(last_lane, 0.0, mid + right))
            put(Y0, x, r0, at(R, x, r0) * (inv * (1.0 / theta)))
            low, mid = mid, high
        return carry

    lax.fori_loop(0, n_tiles + 2, coefficients, 0)

    @pl.when(gx == 0)
    def _():
        FX[XO - 1, pl.ds(YO - 8, rows)] = flat(rows)

    @pl.when(gx == n_gx - 1)
    def _():
        FX[XO + cx - 1, pl.ds(YO - 8, rows)] = flat(rows)

    @pl.when(gy == 0)
    def _():
        for x in range(n_layers):
            FY[x, pl.ds(YO - 1, 1)] = flat(1)

    @pl.when(gy == n_gy - 1)
    def _():
        for x in range(n_layers):
            FY[x, pl.ds(YO + cy - 1, 1)] = flat(1)

    def sweep(src, lo, hi, r0, use):
        prev, cur, f_prev = at(src, lo - 1, r0), at(src, lo, r0), at(FX, lo - 1, r0)
        for x in range(lo, hi):
            nxt, f = at(src, x + 1, r0), at(FX, x, r0)
            fz = at(FZ, x, r0)
            total = f * nxt + f_prev * prev
            total = total + (at(FY, x, r0) * at(src, x, r0 + 1) + at(FY, x, r0 - 1) * at(src, x, r0 - 1))
            total = total + (fz * pltpu.roll(cur, nz - 1, 1) + pltpu.roll(fz * cur, 1, 1))
            use(x, cur, total)
            prev, cur, f_prev = cur, nxt, f

    def in_overlap(row):
        return ((row >= -MARGIN) & (row < MARGIN) & has_lo) | (
            (row >= cy - MARGIN) & (row < cy + MARGIN) & has_hi
        )

    def precondition(y0, y1, z, reach):
        def first(t, carry):
            r0 = tile_row(t)

            def use(x, value, total):
                put(y1, x, r0, A1 * value + B1 * (at(INV, x, r0) * total))

            sweep(y0, -reach - 1, cx + reach + 1, r0, use)
            return carry

        lax.fori_loop(0, n_tiles + 2, first, 0)

        edges = [(MARGIN - 1, 1, m_lo), (cx - MARGIN, -1, m_hi)]
        if reach == MARGIN:
            edges += [(-MARGIN, -1, one), (cx + MARGIN - 1, 1, one)]

        def second(t, carry):
            r0 = tile_row(t)
            row = sub + (r0 - YO)
            over = jnp.where(in_overlap(row), one, 0.0)
            pair_up = 1.0 + over * jnp.where(in_overlap(row + 1), one, 0.0)
            pair_down = 1.0 + over * jnp.where(in_overlap(row - 1), one, 0.0)
            times = 1.0 + over
            t_lo, t_hi = times * (1.0 + m_lo), times * (1.0 + m_hi)
            fixes = {}

            def cut(x, value):
                fixes[x] = value if x not in fixes else fixes[x] + value

            for a, d, weight in edges:
                def face(row0):
                    return at(FX, a if d > 0 else a - 1, row0)

                def e_at(row0):
                    return B1 * (at(INV, a, row0) * (face(row0) * at(y0, a + d, row0)))

                e, e_up, e_down = e_at(r0), e_at(r0 + 1), e_at(r0 - 1)
                fz, inv = at(FZ, a, r0), at(INV, a, r0)
                flow = face(r0) * at(y1, a + d, r0) + (
                    fz * pltpu.roll(e, nz - 1, 1) + pltpu.roll(fz * e, 1, 1)
                )
                side = at(FY, a, r0) * (pair_up * e_up) + at(FY, a, r0 - 1) * (pair_down * e_down)
                cut(a, weight * (times * (A2 * e + B2 * (inv * flow)) + B2 * (inv * side)))
                inner = at(FX, a - 1 if d > 0 else a, r0)
                cut(a - d, (weight * B2) * (times * (at(INV, a - d, r0) * (inner * e))))

            def use(x, value, total):
                y2 = A2 * value + A0 * at(y0, x, r0) + B2 * (at(INV, x, r0) * total)
                scale = t_lo if x < MARGIN else (t_hi if x >= cx - MARGIN else times)
                out = scale * y2
                if x in fixes:
                    out = out - fixes[x]
                put(z, x, r0, out)

            sweep(y1, -reach, cx + reach, r0, use)
            return carry

        lax.fori_loop(0, n_tiles + 2, second, 0)

        def over_x(x):
            if -MARGIN <= x < MARGIN:
                return m_lo
            if cx - MARGIN <= x < cx + MARGIN:
                return m_hi
            return 0.0

        def up(v):
            return pltpu.roll(v, 7, 0)

        def down(v):
            return pltpu.roll(v, 1, 0)

        sides = [(YO, 1, n_lo), (YO + cy - 8, -1, n_hi)]
        if reach == MARGIN:
            sides += [(YO - 8, -1, one), (YO + cy, 1, one)]
        for r0, d, weight in sides:
            edge = sub == (3 if d > 0 else 4)
            inner = sub == (2 if d > 0 else 5)

            def cross(fy, v):
                return fy * up(v) if d > 0 else down(fy * v)

            def e_of(x):
                return jnp.where(edge, B1 * (at(INV, x, r0) * cross(at(FY, x, r0), at(y0, x, r0))), 0.0)

            prev, cur, f_prev = e_of(-reach - 1), e_of(-reach), at(FX, -reach - 1, r0)
            for x in range(-reach, cx + reach):
                nxt, f = e_of(x + 1), at(FX, x, r0)
                fy, fz, inv = at(FY, x, r0), at(FZ, x, r0), at(INV, x, r0)
                times = 1.0 + over_x(x)
                flow = jnp.where(edge, cross(fy, at(y1, x, r0)), 0.0)
                flow = flow + jnp.where(inner, cross(fy, cur), 0.0)
                flow = flow + (fz * pltpu.roll(cur, nz - 1, 1) + pltpu.roll(fz * cur, 1, 1))
                side = (1.0 + over_x(x) * over_x(x + 1)) * (f * nxt) if x + 1 != MARGIN and x + 1 != cx - MARGIN else f * nxt
                side = side + (
                    (1.0 + over_x(x) * over_x(x - 1)) * (f_prev * prev)
                    if x != MARGIN and x != cx - MARGIN else f_prev * prev
                )
                fix = times * (A2 * cur + B2 * (inv * flow)) + B2 * (inv * side)
                put(z, x, r0, at(z, x, r0) - weight * fix)
                prev, cur, f_prev = cur, nxt, f

    zero = jnp.zeros((8, nz), jnp.float32)
    precondition(Y0, Y1, Z0, MARGIN)

    def own_row(t):
        return pl.multiple_of(YO + 8 * t, 8)

    def image0(r0, inside, carry):
        rz, zw = carry

        def use(x, value, total):
            nonlocal rz, zw
            half = 0.5 * total
            put(Y0B, x, r0, (value - at(INV, x, r0) * half) * (1.0 / theta))
            if inside and 0 <= x < cx:
                w = at(DIAG, x, r0) * value - half
                put(W0, x - XO, r0 - YO, w)
                rz = rz + at(R, x, r0) * value
                zw = zw + value * w

        sweep(Z0, -3, cx + 3, r0, use)
        return rz, zw

    rz, zw = lax.fori_loop(0, n_tiles, lambda t, c: image0(own_row(t), True, c), (zero, zero))
    lax.fori_loop(0, 2, lambda t, c: image0(pl.multiple_of(YO - 8 + (cy + 8) * t, 8), False, c), (zero, zero))

    precondition(Y0B, Y1, Z1, 1)

    def image1(t, carry):
        r0 = own_row(t)
        rz1, wz1, zw1, z1w1 = carry

        def use(x, value, total):
            nonlocal rz1, wz1, zw1, z1w1
            w = at(DIAG, x, r0) * value - 0.5 * total
            put(W1, x - XO, r0 - YO, w)
            rz1 = rz1 + at(R, x, r0) * value
            wz1 = wz1 + at(W0, x - XO, r0 - YO) * value
            zw1 = zw1 + at(Z0, x, r0) * w
            z1w1 = z1w1 + value * w

        sweep(Z1, 0, cx, r0, use)
        return rz1, wz1, zw1, z1w1

    rz1, wz1, zw1, z1w1 = lax.fori_loop(0, n_tiles, image1, (zero,) * 4)

    mine = zero
    for q, acc in enumerate((rz, zw, rz1, wz1, zw1, z1w1)):
        mine = jnp.where(sub == q, jnp.sum(acc, axis=0, keepdims=True), mine)
    part[0] = mine
    base = 0
    sent = []
    for s, dims in enumerate(STAGES):
        offs = offsets(dims)
        for n, off in enumerate(offs):
            pltpu.make_async_remote_copy(
                part.at[s], slots.at[base + n], ar_send.at[s], ar_recv.at[s],
                device_id=partner(gx, gy, dims, off), device_id_type=MESH,
            ).start()
        group = slots.at[pl.ds(base, len(offs))]
        both = pltpu.make_async_remote_copy(
            group, group, ar_send.at[s], ar_recv.at[s],
            device_id=partner(gx, gy, dims, offs[0]), device_id_type=MESH,
        )
        both.wait_recv()
        sent.append(both)
        part[s + 1] = part[s] + jnp.sum(slots[base : base + len(offs)], axis=0)
        base += len(offs)
    totals = jnp.sum(part[len(STAGES)], axis=1, keepdims=True)
    rz, zw, rz1, wz1, zw1, z1w1 = [totals[q : q + 1] for q in range(6)]
    step0 = rz / zw
    next_rz = rz - step0 * (rz1 + zw) + step0 * step0 * wz1
    grow = 1.0 + next_rz / rz
    curve = grow * grow * zw - grow * step0 * (zw1 + wz1) + step0 * step0 * z1w1
    step1 = next_rz / curve
    g0 = jnp.broadcast_to(step0 + step1 * grow, (8, nz))
    g1 = jnp.broadcast_to(step1 * step0, (8, nz))

    def finish(x, carry):
        for t in range(n_tiles):
            r0 = YO + 8 * t
            z0, z1 = at(Z0, x, r0), at(Z1, x, r0)
            w0, w1 = at(W0, x - XO, r0 - YO), at(W1, x - XO, r0 - YO)
            put(W0, x - XO, r0 - YO, g0 * z0 - g1 * z1)
            put(W1, x - XO, r0 - YO, at(R, x, r0) - g0 * w0 + g1 * w1)
        pltpu.make_async_copy(W0.at[x], sol_hbm.at[x], out_sem.at[0]).start()
        pltpu.make_async_copy(W1.at[x], res_hbm.at[x], out_sem.at[1]).start()
        return carry

    lax.fori_loop(0, cx, finish, 0)
    pltpu.make_async_copy(W0, sol_hbm, out_sem.at[0]).wait()
    pltpu.make_async_copy(W1, res_hbm, out_sem.at[1]).wait()
    for both in sent:
        both.wait_send()
    for k, (dx, dy) in enumerate(NEAR):

        @pl.when(here(dx, dy))
        def _():
            for copy in halo_copies(k, dx, dy):
                copy.wait_send()


def shards(right_side, conductivity):
    cx, cy, nz = right_side.shape
    ext = pltpu.VMEM((cx + 2 * KW, cy + 2 * YO, nz), jnp.float32)
    own = pltpu.VMEM((cx, cy, nz), jnp.float32)
    dma = pltpu.SemaphoreType.DMA
    any_space = pl.BlockSpec(memory_space=pl.ANY)
    out = jax.ShapeDtypeStruct((cx, cy, nz), jnp.float32)
    return pl.pallas_call(
        kernel,
        out_shape=(out, out),
        in_specs=[any_space, any_space],
        out_specs=(any_space, any_space),
        scratch_shapes=[ext] * 12 + [own] * 2
        + [
            pltpu.VMEM((len(STAGES) + 1, 8, nz), jnp.float32),
            pltpu.VMEM((N_SLOTS, 8, nz), jnp.float32),
            dma((2,)), dma((2,)), dma((16,)), dma((16,)), dma((len(STAGES),)), dma((len(STAGES),)),
        ],
        compiler_params=pltpu.CompilerParams(
            collective_id=0, has_side_effects=True, vmem_limit_bytes=48 << 20
        ),
    )(right_side, conductivity)


def solution(mesh):
    spec = P("gx", "gy", None)
    return jax.shard_map(
        shards, mesh=mesh, in_specs=(spec, spec), out_specs=(spec, spec), check_vma=False
    )
```

```python
import itertools

import jax
import jax.numpy as jnp
from jax import lax
from jax.experimental import pallas as pl
from jax.experimental.pallas import tpu as pltpu
from jax.sharding import PartitionSpec as P

MESH = pl.DeviceIdType.MESH
MARGIN = 4
absorb = 0.05
theta = 1.05
delta = 0.95

sig = theta / delta
rho0 = 1.0 / sig
rho1 = 1.0 / (2.0 * sig - rho0)
rho2 = 1.0 / (2.0 * sig - rho1)
c1, c2 = rho1 * rho0, 2.0 * rho1 / delta
c3, c4 = rho2 * rho1, 2.0 * rho2 / delta
A1 = 1.0 + c1 + c2 * (theta - 1.0)
B1 = 0.5 * c2
A2 = 1.0 + c3 - c4
A0 = c4 * theta - c3
B2 = 0.5 * c4

KW, RW = 7, 6
GUARD = 8
YO = 16
XO = KW

SIZES = dict(c=2, x=4, z=4, y=4, h=2)
STAGES = (("c",), ("x", "y"), ("z", "h"))
NEAR = tuple((dx, dy) for dx in (-1, 0, 1) for dy in (-1, 0, 1) if (dx, dy) != (0, 0))


def offsets(dims):
    return [o for o in itertools.product(*[range(SIZES[d]) for d in dims]) if any(o)]


N_SLOTS = sum(len(offsets(dims)) for dims in STAGES)


def partner(gx, gy, dims, off):
    me = dict(c=gx % 2, x=(gx // 2) % 4, z=gx // 8, y=gy % 4, h=gy // 4)
    for d, o in zip(dims, off):
        me[d] = (me[d] + o) % SIZES[d]
    return (me["z"] * 8 + me["x"] * 2 + me["c"], me["h"] * 4 + me["y"])


def kernel(
    r_hbm, k_hbm, sol, res,
    K, R, INV, DIAG, FX, FY, FZ, Y0, Y1, Y0B, Z0, Z1, W0, W1, part, slots,
    load_sem, send_sem, recv_sem, ar_send, ar_recv,
):
    cx, cy, nz = r_hbm.shape
    n_gx, n_gy = lax.axis_size("gx"), lax.axis_size("gy")
    gx, gy = lax.axis_index("gx"), lax.axis_index("gy")
    full, brick = cy + 16, cy
    strip = 48 if full % 48 == 0 else 8
    own_strip = 64 if brick % 64 == 0 else 8

    def here(dx, dy):
        return (gx + dx >= 0) & (gx + dx < n_gx) & (gy + dy >= 0) & (gy + dy < n_gy)

    own = (pl.ds(XO, cx), pl.ds(YO, cy))
    loads = [
        pltpu.make_async_copy(k_hbm, K.at[own], load_sem.at[0]),
        pltpu.make_async_copy(r_hbm, R.at[own], load_sem.at[1]),
    ]
    for load in loads:
        load.start()

    barrier = pltpu.get_barrier_semaphore()
    count = 0
    for dx, dy in NEAR:
        count = count + here(dx, dy).astype(jnp.int32)

        @pl.when(here(dx, dy))
        def _():
            pl.semaphore_signal(barrier, inc=1, device_id=(gx + dx, gy + dy), device_id_type=MESH)

    for dims in STAGES:
        for off in offsets(dims):
            pl.semaphore_signal(
                barrier, inc=1, device_id=partner(gx, gy, dims, off), device_id_type=MESH
            )
            count = count + 1

    pl.semaphore_wait(barrier, count)

    def halo_copies(k, dx, dy):
        out = []
        for n, (src, dst, width) in enumerate(((k_hbm, K, KW), (r_hbm, R, RW))):
            if dx > 0:
                sx, tx = pl.ds(cx - width, width), pl.ds(XO - width, width)
            elif dx < 0:
                sx, tx = pl.ds(0, width), pl.ds(XO + cx, width)
            else:
                sx, tx = pl.ds(0, cx), pl.ds(XO, cx)
            if dy > 0:
                sy, ty = pl.ds(cy - 8, 8), pl.ds(YO - 8, 8)
            elif dy < 0:
                sy, ty = pl.ds(0, 8), pl.ds(YO + cy, 8)
            else:
                sy, ty = pl.ds(0, cy), pl.ds(YO, cy)
            out.append(
                pltpu.make_async_remote_copy(
                    src.at[sx, sy], dst.at[tx, ty], send_sem.at[2 * k + n], recv_sem.at[2 * k + n],
                    device_id=(gx + dx, gy + dy), device_id_type=MESH,
                )
            )
        return out

    for k, (dx, dy) in enumerate(NEAR):

        @pl.when(here(dx, dy))
        def _():
            for copy in halo_copies(k, dx, dy):
                copy.start()

    rows = cy + 16
    flat = lambda n: jnp.zeros((n, nz), jnp.float32)

    @pl.when(gx == 0)
    def _():
        for x in range(XO):
            K[x, pl.ds(YO - 8, rows)] = flat(rows)
            R[x, pl.ds(YO - 8, rows)] = flat(rows)

    @pl.when(gx == n_gx - 1)
    def _():
        for x in range(XO + cx, XO + cx + KW):
            K[x, pl.ds(YO - 8, rows)] = flat(rows)
            R[x, pl.ds(YO - 8, rows)] = flat(rows)

    for load in loads:
        load.wait()
    for k, (dx, dy) in enumerate(NEAR):

        @pl.when(here(-dx, -dy))
        def _():
            for copy in halo_copies(k, dx, dy):
                copy.wait_recv()

    @pl.when(gx == 0)
    def _():
        K[XO - 1, pl.ds(YO - 8, rows)] = K[XO, pl.ds(YO - 8, rows)]

    @pl.when(gx == n_gx - 1)
    def _():
        K[XO + cx, pl.ds(YO - 8, rows)] = K[XO + cx - 1, pl.ds(YO - 8, rows)]

    n_layers = cx + 2 * KW

    @pl.when(gy == 0)
    def _():
        for x in range(n_layers):
            K[x, pl.ds(YO - 8, 8)] = jnp.broadcast_to(K[x, pl.ds(YO, 1)], (8, nz))
            R[x, pl.ds(YO - 8, 8)] = flat(8)

    @pl.when(gy == n_gy - 1)
    def _():
        for x in range(n_layers):
            K[x, pl.ds(YO + cy, 8)] = jnp.broadcast_to(K[x, pl.ds(YO + cy - 1, 1)], (8, nz))
            R[x, pl.ds(YO + cy, 8)] = flat(8)

    lane = lax.broadcasted_iota(jnp.int32, (strip, nz), 1)
    line = lax.broadcasted_iota(jnp.int32, (strip, nz), 0)
    sub = lax.broadcasted_iota(jnp.int32, (8, nz), 0)
    first_lane, last_lane = lane == 0, lane == nz - 1
    one = jnp.float32(1.0)
    m_lo = jnp.where(gx > 0, one, 0.0)
    m_hi = jnp.where(gx < n_gx - 1, one, 0.0)
    has_lo, has_hi = gy > 0, gy < n_gy - 1
    n_lo = jnp.where(has_lo, one, 0.0)
    n_hi = jnp.where(has_hi, one, 0.0)

    def at(ref, x, row, h=strip):
        return ref[x + XO, pl.ds(row, h), :]

    def put(ref, x, row, value):
        ref[x + XO, pl.ds(row, value.shape[0]), :] = value

    def strip_row(t):
        return pl.multiple_of(YO - 8 + strip * t, 8)

    def strips(body):
        lax.fori_loop(0, full // strip, lambda t, c: body(strip_row(t), c), 0)

    def coefficients(r0, carry):
        low, mid = at(K, -RW - 1, r0), at(K, -RW, r0)
        for x in range(-RW, cx + RW):
            high = at(K, x + 1, r0)
            up, down = at(K, x, r0 + 1), at(K, x, r0 - 1)
            right = jnp.where(last_lane, mid, pltpu.roll(mid, nz - 1, 1))
            left = jnp.where(first_lane, mid, pltpu.roll(mid, 1, 1))
            diag = (absorb + 3.0 * mid) + 0.5 * ((low + high) + (up + down) + (left + right))
            inv = 1.0 / diag
            put(DIAG, x, r0, diag)
            put(INV, x, r0, inv)
            put(FX, x, r0, mid + high)
            put(FY, x, r0, mid + up)
            put(FZ, x, r0, jnp.where(last_lane, 0.0, mid + right))
            put(Y0, x, r0, at(R, x, r0) * (inv * (1.0 / theta)))
            low, mid = mid, high
        return carry

    strips(coefficients)

    @pl.when(gx == 0)
    def _():
        FX[XO - 1, pl.ds(YO - 8, rows)] = flat(rows)

    @pl.when(gx == n_gx - 1)
    def _():
        FX[XO + cx - 1, pl.ds(YO - 8, rows)] = flat(rows)

    @pl.when(gy == 0)
    def _():
        for x in range(n_layers):
            FY[x, pl.ds(YO - 1, 1)] = flat(1)

    @pl.when(gy == n_gy - 1)
    def _():
        for x in range(n_layers):
            FY[x, pl.ds(YO + cy - 1, 1)] = flat(1)

    def sweep(src, lo, hi, r0, use, h=strip):
        prev, cur, f_prev = at(src, lo - 1, r0, h), at(src, lo, r0, h), at(FX, lo - 1, r0, h)
        for x in range(lo, hi):
            nxt, f = at(src, x + 1, r0, h), at(FX, x, r0, h)
            fz = at(FZ, x, r0, h)
            total = f * nxt + f_prev * prev
            total = total + (
                at(FY, x, r0, h) * at(src, x, r0 + 1, h) + at(FY, x, r0 - 1, h) * at(src, x, r0 - 1, h)
            )
            total = total + (fz * pltpu.roll(cur, nz - 1, 1) + pltpu.roll(fz * cur, 1, 1))
            use(x, cur, total)
            prev, cur, f_prev = cur, nxt, f

    def in_overlap(row):
        return ((row >= -MARGIN) & (row < MARGIN) & has_lo) | (
            (row >= cy - MARGIN) & (row < cy + MARGIN) & has_hi
        )

    def precondition(y0, y1, z, reach):
        def first(r0, carry):
            def use(x, value, total):
                put(y1, x, r0, A1 * value + B1 * (at(INV, x, r0) * total))

            sweep(y0, -reach - 1, cx + reach + 1, r0, use)
            return carry

        strips(first)

        edges = [(MARGIN - 1, 1, m_lo), (cx - MARGIN, -1, m_hi)]
        if reach == MARGIN:
            edges += [(-MARGIN, -1, one), (cx + MARGIN - 1, 1, one)]

        def counts(r0):
            row = line + (r0 - YO)
            over = jnp.where(in_overlap(row), one, 0.0)
            return row, over, 1.0 + over

        def second(r0, carry):
            _, _, times = counts(r0)

            def use(x, value, total):
                y2 = A2 * value + A0 * at(y0, x, r0) + B2 * (at(INV, x, r0) * total)
                weight = 1.0 + m_lo if x < MARGIN else (1.0 + m_hi if x >= cx - MARGIN else one)
                put(z, x, r0, (weight * times) * y2)

            sweep(y1, -reach, cx + reach, r0, use)
            return carry

        strips(second)

        def cut_edges(r0, carry):
            row, over, times = counts(r0)
            pair_up = 1.0 + over * jnp.where(in_overlap(row + 1), one, 0.0)
            pair_down = 1.0 + over * jnp.where(in_overlap(row - 1), one, 0.0)
            for a, d, weight in edges:
                def face(row0):
                    return at(FX, a if d > 0 else a - 1, row0)

                def e_at(row0):
                    return B1 * (at(INV, a, row0) * (face(row0) * at(y0, a + d, row0)))

                e, e_up, e_down = e_at(r0), e_at(r0 + 1), e_at(r0 - 1)
                fz, inv = at(FZ, a, r0), at(INV, a, r0)
                flow = face(r0) * at(y1, a + d, r0) + (
                    fz * pltpu.roll(e, nz - 1, 1) + pltpu.roll(fz * e, 1, 1)
                )
                side = at(FY, a, r0) * (pair_up * e_up) + at(FY, a, r0 - 1) * (pair_down * e_down)
                fix = times * (A2 * e + B2 * (inv * flow)) + B2 * (inv * side)
                put(z, a, r0, at(z, a, r0) - weight * fix)
                inner = at(FX, a - 1 if d > 0 else a, r0)
                fix = (weight * B2) * (times * (at(INV, a - d, r0) * (inner * e)))
                put(z, a - d, r0, at(z, a - d, r0) - fix)
            return carry

        strips(cut_edges)

        def over_x(x):
            if -MARGIN <= x < MARGIN:
                return m_lo
            if cx - MARGIN <= x < cx + MARGIN:
                return m_hi
            return 0.0

        def up(v):
            return pltpu.roll(v, 7, 0)

        def down(v):
            return pltpu.roll(v, 1, 0)

        sides = [(YO, 1, n_lo), (YO + cy - 8, -1, n_hi)]
        if reach == MARGIN:
            sides += [(YO - 8, -1, one), (YO + cy, 1, one)]
        for r0, d, weight in sides:
            edge = sub == (3 if d > 0 else 4)
            inner = sub == (2 if d > 0 else 5)

            def cross(fy, v):
                return fy * up(v) if d > 0 else down(fy * v)

            def e_of(x):
                return jnp.where(edge, B1 * (at(INV, x, r0, 8) * cross(at(FY, x, r0, 8), at(y0, x, r0, 8))), 0.0)

            prev, cur, f_prev = e_of(-reach - 1), e_of(-reach), at(FX, -reach - 1, r0, 8)
            for x in range(-reach, cx + reach):
                nxt, f = e_of(x + 1), at(FX, x, r0, 8)
                fy, fz, inv = at(FY, x, r0, 8), at(FZ, x, r0, 8), at(INV, x, r0, 8)
                times = 1.0 + over_x(x)
                flow = jnp.where(edge, cross(fy, at(y1, x, r0, 8)), 0.0)
                flow = flow + jnp.where(inner, cross(fy, cur), 0.0)
                flow = flow + (fz * pltpu.roll(cur, nz - 1, 1) + pltpu.roll(fz * cur, 1, 1))
                side = (1.0 + over_x(x) * over_x(x + 1)) * (f * nxt) if x + 1 != MARGIN and x + 1 != cx - MARGIN else f * nxt
                side = side + (
                    (1.0 + over_x(x) * over_x(x - 1)) * (f_prev * prev)
                    if x != MARGIN and x != cx - MARGIN else f_prev * prev
                )
                fix = times * (A2 * cur + B2 * (inv * flow)) + B2 * (inv * side)
                put(z, x, r0, at(z, x, r0, 8) - weight * fix)
                prev, cur, f_prev = cur, nxt, f

    zero = jnp.zeros((8, nz), jnp.float32)
    precondition(Y0, Y1, Z0, MARGIN)

    def image0(r0, carry):
        def use(x, value, total):
            half = 0.5 * total
            put(Y0B, x, r0, (value - at(INV, x, r0) * half) * (1.0 / theta))
            if 0 <= x < cx:
                put(W0, x - XO, r0 - (YO - 8), at(DIAG, x, r0) * value - half)

        sweep(Z0, -3, cx + 3, r0, use)
        return carry

    strips(image0)
    precondition(Y0B, Y1, Z1, 1)

    def image1(t, carry):
        r0 = pl.multiple_of(YO + own_strip * t, 8)
        sums = list(carry)

        def use(x, value, total):
            w1 = at(DIAG, x, r0, own_strip) * value - 0.5 * total
            put(W1, x - XO, r0 - YO, w1)
            r, z0 = at(R, x, r0, own_strip), at(Z0, x, r0, own_strip)
            w0 = at(W0, x - XO, r0 - (YO - 8), own_strip)
            for q, (a, b) in enumerate(((r, z0), (z0, w0), (r, value), (w0, value), (z0, w1), (value, w1))):
                sums[q] = sums[q] + jnp.sum((a * b).reshape(own_strip // 8, 8, nz), axis=0)

        sweep(Z1, 0, cx, r0, use, own_strip)
        return tuple(sums)

    sums = lax.fori_loop(0, brick // own_strip, image1, (zero,) * 6)

    mine = zero
    for q, acc in enumerate(sums):
        mine = jnp.where(sub == q, jnp.sum(acc, axis=0, keepdims=True), mine)
    part[0] = mine
    base = 0
    sent = []
    for s, dims in enumerate(STAGES):
        offs = offsets(dims)
        for n, off in enumerate(offs):
            pltpu.make_async_remote_copy(
                part.at[s], slots.at[base + n], ar_send.at[s], ar_recv.at[s],
                device_id=partner(gx, gy, dims, off), device_id_type=MESH,
            ).start()
        group = slots.at[pl.ds(base, len(offs))]
        both = pltpu.make_async_remote_copy(
            group, group, ar_send.at[s], ar_recv.at[s],
            device_id=partner(gx, gy, dims, offs[0]), device_id_type=MESH,
        )
        both.wait_recv()
        sent.append(both)
        part[s + 1] = part[s] + jnp.sum(slots[base : base + len(offs)], axis=0)
        base += len(offs)
    totals = jnp.sum(part[len(STAGES)], axis=1, keepdims=True)
    rz, zw, rz1, wz1, zw1, z1w1 = [totals[q : q + 1] for q in range(6)]
    step0 = rz / zw
    next_rz = rz - step0 * (rz1 + zw) + step0 * step0 * wz1
    grow = 1.0 + next_rz / rz
    curve = grow * grow * zw - grow * step0 * (zw1 + wz1) + step0 * step0 * z1w1
    step1 = next_rz / curve
    g0, g1 = step0 + step1 * grow, step1 * step0
    g0 = jnp.broadcast_to(g0, (brick, nz))
    g1 = jnp.broadcast_to(g1, (brick, nz))

    def finish(x, carry):
        z0, z1 = at(Z0, x, YO, brick), at(Z1, x, YO, brick)
        w0, w1 = at(W0, x - XO, 8, brick), at(W1, x - XO, 0, brick)
        sol[x] = g0 * z0 - g1 * z1
        res[x] = at(R, x, YO, brick) - g0 * w0 + g1 * w1
        return carry

    lax.fori_loop(0, cx, finish, 0)
    for both in sent:
        both.wait_send()
    for k, (dx, dy) in enumerate(NEAR):

        @pl.when(here(dx, dy))
        def _():
            for copy in halo_copies(k, dx, dy):
                copy.wait_send()


def shards(right_side, conductivity):
    cx, cy, nz = right_side.shape
    ext = pltpu.VMEM((cx + 2 * KW, cy + 2 * YO, nz), jnp.float32)
    dma = pltpu.SemaphoreType.DMA
    hbm = pl.BlockSpec(memory_space=pltpu.MemorySpace.HBM)
    out = jax.ShapeDtypeStruct((cx, cy, nz), jnp.float32)
    right_side, conductivity = (
        pltpu.with_memory_space_constraint(v, pltpu.MemorySpace.HBM) for v in (right_side, conductivity)
    )
    return pl.pallas_call(
        kernel,
        out_shape=(out, out),
        in_specs=[hbm, hbm],
        out_specs=(pl.BlockSpec(memory_space=pltpu.MemorySpace.VMEM),) * 2,
        scratch_shapes=[ext] * 12
        + [
            pltpu.VMEM((cx, cy + 16, nz), jnp.float32),
            pltpu.VMEM((cx, cy, nz), jnp.float32),
            pltpu.VMEM((len(STAGES) + 1, 8, nz), jnp.float32),
            pltpu.VMEM((N_SLOTS, 8, nz), jnp.float32),
            dma((2,)), dma((16,)), dma((16,)), dma((len(STAGES),)), dma((len(STAGES),)),
        ],
        compiler_params=pltpu.CompilerParams(
            collective_id=0, has_side_effects=True, vmem_limit_bytes=40 << 20
        ),
    )(right_side, conductivity)


def solution(mesh):
    spec = P("gx", "gy", None)
    return jax.shard_map(
        shards, mesh=mesh, in_specs=(spec, spec), out_specs=(spec, spec), check_vma=False
    )
```

```python
import itertools

import jax
import jax.numpy as jnp
from jax import lax
from jax.experimental import pallas as pl
from jax.experimental.pallas import tpu as pltpu
from jax.sharding import PartitionSpec as P

MESH = pl.DeviceIdType.MESH
MARGIN = 4
absorb = 0.05
theta = 1.05
delta = 0.95

sig = theta / delta
rho0 = 1.0 / sig
rho1 = 1.0 / (2.0 * sig - rho0)
rho2 = 1.0 / (2.0 * sig - rho1)
c1, c2 = rho1 * rho0, 2.0 * rho1 / delta
c3, c4 = rho2 * rho1, 2.0 * rho2 / delta
A1 = 1.0 + c1 + c2 * (theta - 1.0)
B1 = 0.5 * c2
A2 = 1.0 + c3 - c4
A0 = c4 * theta - c3
B2 = 0.5 * c4

KW, RW = 7, 6
GUARD = 8
YO = 16
XO = KW

SIZES = dict(c=2, x=4, y=4, z=8)
STAGES = (("c",), ("x", "y"), ("z",))
CORNERS = ((-1, -1), (-1, 1), (1, -1), (1, 1))
NEAR = CORNERS + ((0, -1), (0, 1), (-1, 0), (1, 0))


def offsets(dims):
    def hops(off):
        return sum(min(o, SIZES[d] - o) for d, o in zip(dims, off))

    every = itertools.product(*[range(SIZES[d]) for d in dims])
    return sorted((off for off in every if any(off)), key=hops, reverse=True)


N_SLOTS = sum(len(offsets(dims)) for dims in STAGES)


def partner(gx, gy, dims, off):
    me = dict(c=gx % 2, x=(gx // 2) % 4, y=gy % 4, z=gx // 8 + 4 * (gy // 4))
    for d, o in zip(dims, off):
        me[d] = (me[d] + o) % SIZES[d]
    return ((me["z"] % 4) * 8 + me["x"] * 2 + me["c"], (me["z"] // 4) * 4 + me["y"])


def triangle(start, width):
    out = []
    for d in range(1, width):
        out.append((d, start, width - d))
        start += width - d
    return out


K_CORNER = triangle(0, KW)
R_CORNER = triangle(sum(n for _, _, n in K_CORNER), RW)
CORNER_ROWS = 40
SIDE = KW + RW


def kernel(
    r_hbm, k_hbm, sol, res,
    K, R, INV, DIAG, FX, FY, FZ, Y0, Y1, Y0B, Z0, Z1, W0, W1, side_out, side_in, corner_out, corner_in, part, slots,
    load_sem, send_sem, recv_sem, ar_send, ar_recv,
):
    cx, cy, nz = r_hbm.shape
    n_gx, n_gy = lax.axis_size("gx"), lax.axis_size("gy")
    gx, gy = lax.axis_index("gx"), lax.axis_index("gy")
    full, brick = cy + 16, cy
    strip = 48 if full % 48 == 0 else 8
    own_strip = 64 if brick % 64 == 0 else 8

    def here(dx, dy):
        return (gx + dx >= 0) & (gx + dx < n_gx) & (gy + dy >= 0) & (gy + dy < n_gy)

    own = (pl.ds(XO, cx), pl.ds(YO, cy))
    loads = [
        pltpu.make_async_copy(k_hbm, K.at[own], load_sem.at[0]),
        pltpu.make_async_copy(r_hbm, R.at[own], load_sem.at[1]),
    ]
    for load in loads:
        load.start()

    barrier = pltpu.get_barrier_semaphore()
    count = 0
    for dx, dy in NEAR:
        count = count + here(dx, dy).astype(jnp.int32)

        @pl.when(here(dx, dy))
        def _():
            pl.semaphore_signal(barrier, inc=1, device_id=(gx + dx, gy + dy), device_id_type=MESH)

    for dims in STAGES:
        for off in offsets(dims):
            pl.semaphore_signal(
                barrier, inc=1, device_id=partner(gx, gy, dims, off), device_id_type=MESH
            )
            count = count + 1

    for load in loads:
        load.wait()

    def pack(x, carry):
        for s, (k_row, r_row) in enumerate(((YO, YO), (YO + cy - KW, YO + cy - RW))):
            side_out[s, pl.ds(SIDE * x, 8)] = K[x + XO, pl.ds(k_row, 8)]
            side_out[s, pl.ds(SIDE * x + KW, 8)] = R[x + XO, pl.ds(r_row, 8)]
        return carry

    lax.fori_loop(0, cx, pack, 0)
    for c, (dx, dy) in enumerate(CORNERS):
        for ref, parts in ((K, K_CORNER), (R, R_CORNER)):
            for d, start, n in parts:
                x = XO + (cx - d if dx > 0 else d - 1)
                corner_out[c, pl.ds(start, 8)] = ref[x, pl.ds(YO + cy - n if dy > 0 else YO, 8)]

    pl.semaphore_wait(barrier, count)

    def halo_copies(k, dx, dy):
        if dx and dy:
            pairs = [(corner_out.at[k, pl.ds(0, CORNER_ROWS)], corner_in.at[k, pl.ds(8, CORNER_ROWS)])]
        elif dy:
            s = (dy + 1) // 2
            pairs = [(side_out.at[s, pl.ds(0, SIDE * cx)], side_in.at[s, pl.ds(8, SIDE * cx)])]
        else:
            pairs = []
            for src, dst, width in ((k_hbm, K, KW), (r_hbm, R, RW)):
                sx = cx - width if dx > 0 else 0
                tx = XO - width if dx > 0 else XO + cx
                pairs.append((src.at[pl.ds(sx, width)], dst.at[pl.ds(tx, width), pl.ds(YO, cy)]))
        return [
            pltpu.make_async_remote_copy(
                src, dst, send_sem.at[2 * k + n], recv_sem.at[2 * k + n],
                device_id=(gx + dx, gy + dy), device_id_type=MESH,
            )
            for n, (src, dst) in enumerate(pairs)
        ]

    for k, (dx, dy) in enumerate(NEAR):

        @pl.when(here(dx, dy))
        def _():
            for copy in halo_copies(k, dx, dy):
                copy.start()

    rows = cy + 16
    flat = lambda n: jnp.zeros((n, nz), jnp.float32)

    @pl.when(gx == 0)
    def _():
        for x in range(XO):
            K[x, pl.ds(YO - 8, rows)] = flat(rows)
            R[x, pl.ds(YO - 8, rows)] = flat(rows)

    @pl.when(gx == n_gx - 1)
    def _():
        for x in range(XO + cx, XO + cx + KW):
            K[x, pl.ds(YO - 8, rows)] = flat(rows)
            R[x, pl.ds(YO - 8, rows)] = flat(rows)

    for k, (dx, dy) in enumerate(NEAR):

        @pl.when(here(-dx, -dy))
        def _():
            for copy in halo_copies(k, dx, dy):
                copy.wait_recv()

    for s, (dy, k_off, r_off) in enumerate(((-1, 8, 8 + KW), (1, 8 + KW - 8, 8 + SIDE - 8))):

        @pl.when(here(0, -dy))
        def _():
            row = YO - 8 if dy > 0 else YO + cy

            def unpack(x, carry):
                K[x + XO, pl.ds(row, 8)] = side_in[s, pl.ds(SIDE * x + k_off, 8)]
                R[x + XO, pl.ds(row, 8)] = side_in[s, pl.ds(SIDE * x + r_off, 8)]
                return carry

            lax.fori_loop(0, cx, unpack, 0)

    for c, (dx, dy) in enumerate(CORNERS):

        @pl.when(here(-dx, -dy))
        def _():
            row = YO - 8 if dy > 0 else YO + cy
            for ref, parts in ((K, K_CORNER), (R, R_CORNER)):
                for d, start, n in parts:
                    x = XO + (-d if dx > 0 else cx + d - 1)
                    ref[x, pl.ds(row, 8)] = corner_in[c, pl.ds(start + (n if dy > 0 else 8), 8)]

    @pl.when(gx == 0)
    def _():
        K[XO - 1, pl.ds(YO - 8, rows)] = K[XO, pl.ds(YO - 8, rows)]

    @pl.when(gx == n_gx - 1)
    def _():
        K[XO + cx, pl.ds(YO - 8, rows)] = K[XO + cx - 1, pl.ds(YO - 8, rows)]

    n_layers = cx + 2 * KW

    @pl.when(gy == 0)
    def _():
        for x in range(n_layers):
            K[x, pl.ds(YO - 8, 8)] = jnp.broadcast_to(K[x, pl.ds(YO, 1)], (8, nz))
            R[x, pl.ds(YO - 8, 8)] = flat(8)

    @pl.when(gy == n_gy - 1)
    def _():
        for x in range(n_layers):
            K[x, pl.ds(YO + cy, 8)] = jnp.broadcast_to(K[x, pl.ds(YO + cy - 1, 1)], (8, nz))
            R[x, pl.ds(YO + cy, 8)] = flat(8)

    lane = lax.broadcasted_iota(jnp.int32, (strip, nz), 1)
    line = lax.broadcasted_iota(jnp.int32, (strip, nz), 0)
    sub = lax.broadcasted_iota(jnp.int32, (8, nz), 0)
    first_lane, last_lane = lane == 0, lane == nz - 1
    one = jnp.float32(1.0)
    m_lo = jnp.where(gx > 0, one, 0.0)
    m_hi = jnp.where(gx < n_gx - 1, one, 0.0)
    has_lo, has_hi = gy > 0, gy < n_gy - 1
    n_lo = jnp.where(has_lo, one, 0.0)
    n_hi = jnp.where(has_hi, one, 0.0)

    def at(ref, x, row, h=strip):
        return ref[x + XO, pl.ds(row, h), :]

    def put(ref, x, row, value):
        ref[x + XO, pl.ds(row, value.shape[0]), :] = value

    def strip_row(t):
        return pl.multiple_of(YO - 8 + strip * t, 8)

    def strips(body):
        lax.fori_loop(0, full // strip, lambda t, c: body(strip_row(t), c), 0)

    def coefficients(r0, carry):
        low, mid = at(K, -RW - 1, r0), at(K, -RW, r0)
        for x in range(-RW, cx + RW):
            high = at(K, x + 1, r0)
            up, down = at(K, x, r0 + 1), at(K, x, r0 - 1)
            right = jnp.where(last_lane, mid, pltpu.roll(mid, nz - 1, 1))
            left = jnp.where(first_lane, mid, pltpu.roll(mid, 1, 1))
            diag = (absorb + 3.0 * mid) + 0.5 * ((low + high) + (up + down) + (left + right))
            inv = 1.0 / diag
            put(DIAG, x, r0, diag)
            put(INV, x, r0, inv)
            put(FX, x, r0, mid + high)
            put(FY, x, r0, mid + up)
            put(FZ, x, r0, jnp.where(last_lane, 0.0, mid + right))
            put(Y0, x, r0, at(R, x, r0) * (inv * (1.0 / theta)))
            low, mid = mid, high
        return carry

    strips(coefficients)

    @pl.when(gx == 0)
    def _():
        FX[XO - 1, pl.ds(YO - 8, rows)] = flat(rows)

    @pl.when(gx == n_gx - 1)
    def _():
        FX[XO + cx - 1, pl.ds(YO - 8, rows)] = flat(rows)

    @pl.when(gy == 0)
    def _():
        for x in range(n_layers):
            FY[x, pl.ds(YO - 1, 1)] = flat(1)

    @pl.when(gy == n_gy - 1)
    def _():
        for x in range(n_layers):
            FY[x, pl.ds(YO + cy - 1, 1)] = flat(1)

    def sweep(src, lo, hi, r0, use, h=strip):
        prev, cur, f_prev = at(src, lo - 1, r0, h), at(src, lo, r0, h), at(FX, lo - 1, r0, h)
        for x in range(lo, hi):
            nxt, f = at(src, x + 1, r0, h), at(FX, x, r0, h)
            fz = at(FZ, x, r0, h)
            total = f * nxt + f_prev * prev
            total = total + (
                at(FY, x, r0, h) * at(src, x, r0 + 1, h) + at(FY, x, r0 - 1, h) * at(src, x, r0 - 1, h)
            )
            total = total + (fz * pltpu.roll(cur, nz - 1, 1) + pltpu.roll(fz * cur, 1, 1))
            use(x, cur, total)
            prev, cur, f_prev = cur, nxt, f

    def in_overlap(row):
        return ((row >= -MARGIN) & (row < MARGIN) & has_lo) | (
            (row >= cy - MARGIN) & (row < cy + MARGIN) & has_hi
        )

    def precondition(y0, y1, z, reach):
        def first(r0, carry):
            def use(x, value, total):
                put(y1, x, r0, A1 * value + B1 * (at(INV, x, r0) * total))

            sweep(y0, -reach - 1, cx + reach + 1, r0, use)
            return carry

        strips(first)

        edges = [(MARGIN - 1, 1, m_lo), (cx - MARGIN, -1, m_hi)]
        if reach == MARGIN:
            edges += [(-MARGIN, -1, one), (cx + MARGIN - 1, 1, one)]

        def counts(r0):
            row = line + (r0 - YO)
            over = jnp.where(in_overlap(row), one, 0.0)
            return row, over, 1.0 + over

        def second(r0, carry):
            _, _, times = counts(r0)

            def use(x, value, total):
                y2 = A2 * value + A0 * at(y0, x, r0) + B2 * (at(INV, x, r0) * total)
                weight = 1.0 + m_lo if x < MARGIN else (1.0 + m_hi if x >= cx - MARGIN else one)
                put(z, x, r0, (weight * times) * y2)

            sweep(y1, -reach, cx + reach, r0, use)
            return carry

        strips(second)

        def cut_edges(r0, carry):
            row, over, times = counts(r0)
            pair_up = 1.0 + over * jnp.where(in_overlap(row + 1), one, 0.0)
            pair_down = 1.0 + over * jnp.where(in_overlap(row - 1), one, 0.0)
            for a, d, weight in edges:
                def face(row0):
                    return at(FX, a if d > 0 else a - 1, row0)

                def e_at(row0):
                    return B1 * (at(INV, a, row0) * (face(row0) * at(y0, a + d, row0)))

                e, e_up, e_down = e_at(r0), e_at(r0 + 1), e_at(r0 - 1)
                fz, inv = at(FZ, a, r0), at(INV, a, r0)
                flow = face(r0) * at(y1, a + d, r0) + (
                    fz * pltpu.roll(e, nz - 1, 1) + pltpu.roll(fz * e, 1, 1)
                )
                side = at(FY, a, r0) * (pair_up * e_up) + at(FY, a, r0 - 1) * (pair_down * e_down)
                fix = times * (A2 * e + B2 * (inv * flow)) + B2 * (inv * side)
                put(z, a, r0, at(z, a, r0) - weight * fix)
                inner = at(FX, a - 1 if d > 0 else a, r0)
                fix = (weight * B2) * (times * (at(INV, a - d, r0) * (inner * e)))
                put(z, a - d, r0, at(z, a - d, r0) - fix)
            return carry

        strips(cut_edges)

        def over_x(x):
            if -MARGIN <= x < MARGIN:
                return m_lo
            if cx - MARGIN <= x < cx + MARGIN:
                return m_hi
            return 0.0

        def up(v):
            return pltpu.roll(v, 7, 0)

        def down(v):
            return pltpu.roll(v, 1, 0)

        sides = [(YO, 1, n_lo), (YO + cy - 8, -1, n_hi)]
        if reach == MARGIN:
            sides += [(YO - 8, -1, one), (YO + cy, 1, one)]
        for r0, d, weight in sides:
            edge = sub == (3 if d > 0 else 4)
            inner = sub == (2 if d > 0 else 5)

            def cross(fy, v):
                return fy * up(v) if d > 0 else down(fy * v)

            def e_of(x):
                return jnp.where(edge, B1 * (at(INV, x, r0, 8) * cross(at(FY, x, r0, 8), at(y0, x, r0, 8))), 0.0)

            prev, cur, f_prev = e_of(-reach - 1), e_of(-reach), at(FX, -reach - 1, r0, 8)
            for x in range(-reach, cx + reach):
                nxt, f = e_of(x + 1), at(FX, x, r0, 8)
                fy, fz, inv = at(FY, x, r0, 8), at(FZ, x, r0, 8), at(INV, x, r0, 8)
                times = 1.0 + over_x(x)
                flow = jnp.where(edge, cross(fy, at(y1, x, r0, 8)), 0.0)
                flow = flow + jnp.where(inner, cross(fy, cur), 0.0)
                flow = flow + (fz * pltpu.roll(cur, nz - 1, 1) + pltpu.roll(fz * cur, 1, 1))
                side = (1.0 + over_x(x) * over_x(x + 1)) * (f * nxt) if x + 1 != MARGIN and x + 1 != cx - MARGIN else f * nxt
                side = side + (
                    (1.0 + over_x(x) * over_x(x - 1)) * (f_prev * prev)
                    if x != MARGIN and x != cx - MARGIN else f_prev * prev
                )
                fix = times * (A2 * cur + B2 * (inv * flow)) + B2 * (inv * side)
                put(z, x, r0, at(z, x, r0, 8) - weight * fix)
                prev, cur, f_prev = cur, nxt, f

    zero = jnp.zeros((8, nz), jnp.float32)
    precondition(Y0, Y1, Z0, MARGIN)

    def image0(r0, carry):
        def use(x, value, total):
            half = 0.5 * total
            put(Y0B, x, r0, (value - at(INV, x, r0) * half) * (1.0 / theta))
            if 0 <= x < cx:
                put(W0, x - XO, r0 - (YO - 8), at(DIAG, x, r0) * value - half)

        sweep(Z0, -3, cx + 3, r0, use)
        return carry

    strips(image0)
    precondition(Y0B, Y1, Z1, 1)

    def image1(t, carry):
        r0 = pl.multiple_of(YO + own_strip * t, 8)
        sums = list(carry)

        def use(x, value, total):
            w1 = at(DIAG, x, r0, own_strip) * value - 0.5 * total
            put(W1, x - XO, r0 - YO, w1)
            r, z0 = at(R, x, r0, own_strip), at(Z0, x, r0, own_strip)
            w0 = at(W0, x - XO, r0 - (YO - 8), own_strip)
            for q, (a, b) in enumerate(((r, z0), (z0, w0), (r, value), (w0, value), (z0, w1), (value, w1))):
                sums[q] = sums[q] + jnp.sum((a * b).reshape(own_strip // 8, 8, nz), axis=0)

        sweep(Z1, 0, cx, r0, use, own_strip)
        return tuple(sums)

    sums = lax.fori_loop(0, brick // own_strip, image1, (zero,) * 6)

    group_of = lax.broadcasted_iota(jnp.int32, (8, nz), 1) // 16
    mine = zero
    for q, acc in enumerate(sums):
        mine = jnp.where(sub == q, jnp.sum(acc, axis=0, keepdims=True), mine)
    for shift in (64, 32, 16):
        mine = mine + pltpu.roll(mine, shift, 1)
    part[0] = jnp.sum(jnp.where(sub == group_of, mine, 0.0), axis=0, keepdims=True)
    base = 0
    sent = []
    for s, dims in enumerate(STAGES):
        offs = offsets(dims)
        for n, off in enumerate(offs):
            pltpu.make_async_remote_copy(
                part.at[s], slots.at[base + n], ar_send.at[s], ar_recv.at[s],
                device_id=partner(gx, gy, dims, off), device_id_type=MESH,
            ).start()
        group = slots.at[pl.ds(base, len(offs))]
        both = pltpu.make_async_remote_copy(
            group, group, ar_send.at[s], ar_recv.at[s],
            device_id=partner(gx, gy, dims, offs[0]), device_id_type=MESH,
        )
        both.wait_recv()
        sent.append(both)
        part[s + 1] = part[s] + jnp.sum(slots[base : base + len(offs)], axis=0)
        base += len(offs)
    totals = jnp.where(sub == group_of, jnp.broadcast_to(part[len(STAGES)], (8, nz)), 0.0)
    totals = jnp.sum(totals, axis=1, keepdims=True)
    rz, zw, rz1, wz1, zw1, z1w1 = [totals[q : q + 1] for q in range(6)]
    step0 = rz / zw
    next_rz = rz - step0 * (rz1 + zw) + step0 * step0 * wz1
    grow = 1.0 + next_rz / rz
    curve = grow * grow * zw - grow * step0 * (zw1 + wz1) + step0 * step0 * z1w1
    step1 = next_rz / curve
    g0, g1 = step0 + step1 * grow, step1 * step0
    g0 = jnp.broadcast_to(g0, (brick, nz))
    g1 = jnp.broadcast_to(g1, (brick, nz))

    def finish(x, carry):
        z0, z1 = at(Z0, x, YO, brick), at(Z1, x, YO, brick)
        w0, w1 = at(W0, x - XO, 8, brick), at(W1, x - XO, 0, brick)
        sol[x] = g0 * z0 - g1 * z1
        res[x] = at(R, x, YO, brick) - g0 * w0 + g1 * w1
        return carry

    lax.fori_loop(0, cx, finish, 0)
    for both in sent:
        both.wait_send()
    for k, (dx, dy) in enumerate(NEAR):

        @pl.when(here(dx, dy))
        def _():
            for copy in halo_copies(k, dx, dy):
                copy.wait_send()


def shards(right_side, conductivity):
    cx, cy, nz = right_side.shape
    ext = pltpu.VMEM((cx + 2 * KW, cy + 2 * YO, nz), jnp.float32)
    dma = pltpu.SemaphoreType.DMA
    hbm = pl.BlockSpec(memory_space=pltpu.MemorySpace.HBM)
    out = jax.ShapeDtypeStruct((cx, cy, nz), jnp.float32)
    right_side, conductivity = (
        pltpu.with_memory_space_constraint(v, pltpu.MemorySpace.HBM) for v in (right_side, conductivity)
    )
    return pl.pallas_call(
        kernel,
        out_shape=(out, out),
        in_specs=[hbm, hbm],
        out_specs=(pl.BlockSpec(memory_space=pltpu.MemorySpace.VMEM),) * 2,
        scratch_shapes=[ext] * 12
        + [
            pltpu.VMEM((cx, cy + 16, nz), jnp.float32),
            pltpu.VMEM((cx, cy, nz), jnp.float32),
            pltpu.VMEM((2, SIDE * cx + 8, nz), jnp.float32),
            pltpu.VMEM((2, SIDE * cx + 16, nz), jnp.float32),
            pltpu.VMEM((4, CORNER_ROWS + 8, nz), jnp.float32),
            pltpu.VMEM((4, CORNER_ROWS + 16, nz), jnp.float32),
            pltpu.VMEM((len(STAGES) + 1, 1, nz), jnp.float32),
            pltpu.VMEM((N_SLOTS, 1, nz), jnp.float32),
            dma((2,)), dma((16,)), dma((16,)), dma((len(STAGES),)), dma((len(STAGES),)),
        ],
        compiler_params=pltpu.CompilerParams(
            collective_id=0, has_side_effects=True, vmem_limit_bytes=40 << 20
        ),
    )(right_side, conductivity)


def solution(mesh):
    spec = P("gx", "gy", None)
    return jax.shard_map(
        shards, mesh=mesh, in_specs=(spec, spec), out_specs=(spec, spec), check_vma=False
    )
```

```python
import itertools

import jax
import jax.numpy as jnp
from jax import lax
from jax.experimental import pallas as pl
from jax.experimental.pallas import tpu as pltpu
from jax.sharding import PartitionSpec as P

MESH = pl.DeviceIdType.MESH
MARGIN = 4
absorb = 0.05
theta = 1.05
delta = 0.95

sig = theta / delta
rho0 = 1.0 / sig
rho1 = 1.0 / (2.0 * sig - rho0)
rho2 = 1.0 / (2.0 * sig - rho1)
c1, c2 = rho1 * rho0, 2.0 * rho1 / delta
c3, c4 = rho2 * rho1, 2.0 * rho2 / delta
A1 = 1.0 + c1 + c2 * (theta - 1.0)
B1 = 0.5 * c2
A2 = 1.0 + c3 - c4
A0 = c4 * theta - c3
B2 = 0.5 * c4

KW, RW = 7, 6
GUARD = 8
YO = 16
XO = KW

SIZES = dict(c=2, x=4, y=4, z=8)
STAGES = (("c",), ("x", "y"), ("z",))
CORNERS = ((-1, -1), (-1, 1), (1, -1), (1, 1))
NEAR = CORNERS + ((0, -1), (0, 1), (-1, 0), (1, 0))


def offsets(dims):
    def hops(off):
        return sum(min(o, SIZES[d] - o) for d, o in zip(dims, off))

    every = itertools.product(*[range(SIZES[d]) for d in dims])
    return sorted((off for off in every if any(off)), key=hops, reverse=True)


N_SLOTS = sum(len(offsets(dims)) for dims in STAGES)


def partner(gx, gy, dims, off):
    me = dict(c=gx % 2, x=(gx // 2) % 4, y=gy % 4, z=gx // 8 + 4 * (gy // 4))
    for d, o in zip(dims, off):
        me[d] = (me[d] + o) % SIZES[d]
    return ((me["z"] % 4) * 8 + me["x"] * 2 + me["c"], (me["z"] // 4) * 4 + me["y"])


def triangle(start, width):
    out = []
    for d in range(1, width):
        out.append((d, start, width - d))
        start += width - d
    return out


K_CORNER = triangle(0, KW)
R_CORNER = triangle(sum(n for _, _, n in K_CORNER), RW)
CORNER_ROWS = 40
SIDE = KW + RW


def kernel(
    r_hbm, k_hbm, sol, res,
    K, R, INV, DIAG, FX, FY, FZ, Y0, Y1, Y0B, Z0, Z1, W0, W1, side_out, side_in, corner_out, corner_in, part, slots,
    load_sem, send_sem, recv_sem, ar_send, ar_recv,
):
    cx, cy, nz = r_hbm.shape
    n_gx, n_gy = lax.axis_size("gx"), lax.axis_size("gy")
    gx, gy = lax.axis_index("gx"), lax.axis_index("gy")
    full, brick = cy + 16, cy
    strip = 48 if full % 48 == 0 else 8
    own_strip = 64 if brick % 64 == 0 else 8

    def here(dx, dy):
        return (gx + dx >= 0) & (gx + dx < n_gx) & (gy + dy >= 0) & (gy + dy < n_gy)

    own = (pl.ds(XO, cx), pl.ds(YO, cy))
    loads = [
        pltpu.make_async_copy(k_hbm, K.at[own], load_sem.at[0]),
        pltpu.make_async_copy(r_hbm, R.at[own], load_sem.at[1]),
    ]
    for load in loads:
        load.start()

    barrier = pltpu.get_barrier_semaphore()
    count = 0
    for dx, dy in NEAR:
        count = count + here(dx, dy).astype(jnp.int32)

        @pl.when(here(dx, dy))
        def _():
            pl.semaphore_signal(barrier, inc=1, device_id=(gx + dx, gy + dy), device_id_type=MESH)

    for dims in STAGES:
        for off in offsets(dims):
            pl.semaphore_signal(
                barrier, inc=1, device_id=partner(gx, gy, dims, off), device_id_type=MESH
            )
            count = count + 1

    for load in loads:
        load.wait()

    def pack(x, carry):
        for s, (k_row, r_row) in enumerate(((YO, YO), (YO + cy - KW, YO + cy - RW))):
            side_out[s, pl.ds(SIDE * x, 8)] = K[x + XO, pl.ds(k_row, 8)]
            side_out[s, pl.ds(SIDE * x + KW, 8)] = R[x + XO, pl.ds(r_row, 8)]
        return carry

    lax.fori_loop(0, cx, pack, 0)
    for c, (dx, dy) in enumerate(CORNERS):
        for ref, parts in ((K, K_CORNER), (R, R_CORNER)):
            for d, start, n in parts:
                x = XO + (cx - d if dx > 0 else d - 1)
                corner_out[c, pl.ds(start, 8)] = ref[x, pl.ds(YO + cy - n if dy > 0 else YO, 8)]

    pl.semaphore_wait(barrier, count)

    def halo_copies(k, dx, dy):
        if dx and dy:
            pairs = [(corner_out.at[k, pl.ds(0, CORNER_ROWS)], corner_in.at[k, pl.ds(8, CORNER_ROWS)])]
        elif dy:
            s = (dy + 1) // 2
            pairs = [(side_out.at[s, pl.ds(0, SIDE * cx)], side_in.at[s, pl.ds(8, SIDE * cx)])]
        else:
            pairs = []
            for src, dst, width in ((k_hbm, K, KW), (r_hbm, R, RW)):
                sx = cx - width if dx > 0 else 0
                tx = XO - width if dx > 0 else XO + cx
                pairs.append((src.at[pl.ds(sx, width)], dst.at[pl.ds(tx, width), pl.ds(YO, cy)]))
        return [
            pltpu.make_async_remote_copy(
                src, dst, send_sem.at[2 * k + n], recv_sem.at[2 * k + n],
                device_id=(gx + dx, gy + dy), device_id_type=MESH,
            )
            for n, (src, dst) in enumerate(pairs)
        ]

    def send(along_x):
        for k, (dx, dy) in enumerate(NEAR):
            if along_x == (dy == 0):

                @pl.when(here(dx, dy))
                def _():
                    for copy in halo_copies(k, dx, dy):
                        copy.start()

    send(False)
    send(True)

    sub = lax.broadcasted_iota(jnp.int32, (8, nz), 0)

    def line_of(h):
        return lax.broadcasted_iota(jnp.int32, (h, nz), 0)

    one = jnp.float32(1.0)
    m_lo = jnp.where(gx > 0, one, 0.0)
    m_hi = jnp.where(gx < n_gx - 1, one, 0.0)
    has_lo, has_hi = gy > 0, gy < n_gy - 1
    n_lo = jnp.where(has_lo, one, 0.0)
    n_hi = jnp.where(has_hi, one, 0.0)

    def at(ref, x, row, h=strip):
        return ref[x + XO, pl.ds(row, h), :]

    def put(ref, x, row, value):
        ref[x + XO, pl.ds(row, value.shape[0]), :] = value

    def strip_row(t):
        return pl.multiple_of(YO - 8 + strip * t, 8)

    def strips(body):
        lax.fori_loop(0, full // strip, lambda t, c: body(strip_row(t), c), 0)

    core, tall = cy - 16, 64 if cy % 64 == 0 else 8
    core_strip = 56 if core % 56 == 0 else 8

    def inside(stage, m):
        def body(t, carry):
            stage(pl.multiple_of(YO + tall * t, 8), m, cx - m, tall)
            return carry

        lax.fori_loop(0, cy // tall, body, 0)

    def around(stage, m, reach):
        def sides(t, carry):
            r0 = pl.multiple_of(YO + 8 + core_strip * t, 8)
            stage(r0, -reach, m, core_strip)
            stage(r0, cx - m, cx + reach, core_strip)
            return carry

        def ends(t, carry):
            stage(pl.multiple_of(YO - 8 + cy * t, 8), -reach, cx + reach, 16)
            return carry

        lax.fori_loop(0, core // core_strip, sides, 0)
        lax.fori_loop(0, 2, ends, 0)

    def coefficients(r0, lo, hi, h):
        lane = lax.broadcasted_iota(jnp.int32, (h, nz), 1)
        first_lane, last_lane = lane == 0, lane == nz - 1
        low, mid = at(K, lo - 1, r0, h), at(K, lo, r0, h)
        for x in range(lo, hi):
            high = at(K, x + 1, r0, h)
            up, down = at(K, x, r0 + 1, h), at(K, x, r0 - 1, h)
            right = jnp.where(last_lane, mid, pltpu.roll(mid, nz - 1, 1))
            left = jnp.where(first_lane, mid, pltpu.roll(mid, 1, 1))
            diag = (absorb + 3.0 * mid) + 0.5 * ((low + high) + (up + down) + (left + right))
            inv = 1.0 / diag
            if 0 <= x < cx:
                put(DIAG, x, r0, diag)
            put(INV, x, r0, inv)
            put(FX, x, r0, mid + high)
            put(FY, x, r0, mid + up)
            put(FZ, x, r0, jnp.where(last_lane, 0.0, mid + right))
            put(Y0, x, r0, at(R, x, r0, h) * (inv * (1.0 / theta)))
            low, mid = mid, high

    def sweep(src, lo, hi, r0, use, h=strip):
        prev, cur, f_prev = at(src, lo - 1, r0, h), at(src, lo, r0, h), at(FX, lo - 1, r0, h)
        for x in range(lo, hi):
            nxt, f = at(src, x + 1, r0, h), at(FX, x, r0, h)
            fz = at(FZ, x, r0, h)
            total = f * nxt + f_prev * prev
            total = total + (
                at(FY, x, r0, h) * at(src, x, r0 + 1, h) + at(FY, x, r0 - 1, h) * at(src, x, r0 - 1, h)
            )
            total = total + (fz * pltpu.roll(cur, nz - 1, 1) + pltpu.roll(fz * cur, 1, 1))
            use(x, cur, total)
            prev, cur, f_prev = cur, nxt, f

    def in_overlap(row):
        return ((row >= -MARGIN) & (row < MARGIN) & has_lo) | (
            (row >= cy - MARGIN) & (row < cy + MARGIN) & has_hi
        )

    def counts(r0, h):
        row = line_of(h) + (r0 - YO)
        over = jnp.where(in_overlap(row), one, 0.0)
        return row, over, 1.0 + over

    def first(y0, y1):
        def stage(r0, lo, hi, h):
            def use(x, value, total):
                put(y1, x, r0, A1 * value + B1 * (at(INV, x, r0, h) * total))

            sweep(y0, lo, hi, r0, use, h)

        return stage

    def second(y0, y1, z):
        def stage(r0, lo, hi, h):
            _, _, times = counts(r0, h)

            def use(x, value, total):
                y2 = A2 * value + A0 * at(y0, x, r0, h) + B2 * (at(INV, x, r0, h) * total)
                weight = 1.0 + m_lo if x < MARGIN else (1.0 + m_hi if x >= cx - MARGIN else one)
                put(z, x, r0, (weight * times) * y2)

            sweep(y1, lo, hi, r0, use, h)

        return stage

    inside(coefficients, 1)
    inside(first(Y0, Y1), 2)
    inside(second(Y0, Y1, Z0), 3)

    rows = cy + 16
    flat = lambda n: jnp.zeros((n, nz), jnp.float32)

    @pl.when(gx == 0)
    def _():
        for x in range(XO):
            K[x, pl.ds(YO - 8, rows)] = flat(rows)
            R[x, pl.ds(YO - 8, rows)] = flat(rows)

    @pl.when(gx == n_gx - 1)
    def _():
        for x in range(XO + cx, XO + cx + KW):
            K[x, pl.ds(YO - 8, rows)] = flat(rows)
            R[x, pl.ds(YO - 8, rows)] = flat(rows)

    for k, (dx, dy) in enumerate(NEAR):

        @pl.when(here(-dx, -dy))
        def _():
            for copy in halo_copies(k, dx, dy):
                copy.wait_recv()

    for s, (dy, k_off, r_off) in enumerate(((-1, 8, 8 + KW), (1, 8 + KW - 8, 8 + SIDE - 8))):

        @pl.when(here(0, -dy))
        def _():
            row = YO - 8 if dy > 0 else YO + cy

            def unpack(x, carry):
                K[x + XO, pl.ds(row, 8)] = side_in[s, pl.ds(SIDE * x + k_off, 8)]
                R[x + XO, pl.ds(row, 8)] = side_in[s, pl.ds(SIDE * x + r_off, 8)]
                return carry

            lax.fori_loop(0, cx, unpack, 0)

    for c, (dx, dy) in enumerate(CORNERS):

        @pl.when(here(-dx, -dy))
        def _():
            row = YO - 8 if dy > 0 else YO + cy
            for ref, parts in ((K, K_CORNER), (R, R_CORNER)):
                for d, start, n in parts:
                    x = XO + (-d if dx > 0 else cx + d - 1)
                    ref[x, pl.ds(row, 8)] = corner_in[c, pl.ds(start + (n if dy > 0 else 8), 8)]

    @pl.when(gx == 0)
    def _():
        K[XO - 1, pl.ds(YO - 8, rows)] = K[XO, pl.ds(YO - 8, rows)]

    @pl.when(gx == n_gx - 1)
    def _():
        K[XO + cx, pl.ds(YO - 8, rows)] = K[XO + cx - 1, pl.ds(YO - 8, rows)]

    n_layers = cx + 2 * KW

    @pl.when(gy == 0)
    def _():
        for x in range(n_layers):
            K[x, pl.ds(YO - 8, 8)] = jnp.broadcast_to(K[x, pl.ds(YO, 1)], (8, nz))
            R[x, pl.ds(YO - 8, 8)] = flat(8)

    @pl.when(gy == n_gy - 1)
    def _():
        for x in range(n_layers):
            K[x, pl.ds(YO + cy, 8)] = jnp.broadcast_to(K[x, pl.ds(YO + cy - 1, 1)], (8, nz))
            R[x, pl.ds(YO + cy, 8)] = flat(8)

    around(coefficients, 1, RW)

    @pl.when(gx == 0)
    def _():
        FX[XO - 1, pl.ds(YO - 8, rows)] = flat(rows)

    @pl.when(gx == n_gx - 1)
    def _():
        FX[XO + cx - 1, pl.ds(YO - 8, rows)] = flat(rows)

    @pl.when(gy == 0)
    def _():
        for x in range(n_layers):
            FY[x, pl.ds(YO - 1, 1)] = flat(1)

    @pl.when(gy == n_gy - 1)
    def _():
        for x in range(n_layers):
            FY[x, pl.ds(YO + cy - 1, 1)] = flat(1)

    around(first(Y0, Y1), 2, MARGIN + 1)
    around(second(Y0, Y1, Z0), 3, MARGIN)

    def precondition(y0, y1, z, reach):
        strips(lambda r0, c: (first(y0, y1)(r0, -reach - 1, cx + reach + 1, strip), c)[1])
        strips(lambda r0, c: (second(y0, y1, z)(r0, -reach, cx + reach, strip), c)[1])
        cut(y0, y1, z, reach)

    def cut(y0, y1, z, reach):
        edges = [(MARGIN - 1, 1, m_lo), (cx - MARGIN, -1, m_hi)]
        if reach == MARGIN:
            edges += [(-MARGIN, -1, one), (cx + MARGIN - 1, 1, one)]

        def cut_edges(r0, carry):
            row, over, times = counts(r0, strip)
            pair_up = 1.0 + over * jnp.where(in_overlap(row + 1), one, 0.0)
            pair_down = 1.0 + over * jnp.where(in_overlap(row - 1), one, 0.0)
            for a, d, weight in edges:
                def face(row0):
                    return at(FX, a if d > 0 else a - 1, row0)

                def e_at(row0):
                    return B1 * (at(INV, a, row0) * (face(row0) * at(y0, a + d, row0)))

                e, e_up, e_down = e_at(r0), e_at(r0 + 1), e_at(r0 - 1)
                fz, inv = at(FZ, a, r0), at(INV, a, r0)
                flow = face(r0) * at(y1, a + d, r0) + (
                    fz * pltpu.roll(e, nz - 1, 1) + pltpu.roll(fz * e, 1, 1)
                )
                side = at(FY, a, r0) * (pair_up * e_up) + at(FY, a, r0 - 1) * (pair_down * e_down)
                fix = times * (A2 * e + B2 * (inv * flow)) + B2 * (inv * side)
                put(z, a, r0, at(z, a, r0) - weight * fix)
                inner = at(FX, a - 1 if d > 0 else a, r0)
                fix = (weight * B2) * (times * (at(INV, a - d, r0) * (inner * e)))
                put(z, a - d, r0, at(z, a - d, r0) - fix)
            return carry

        strips(cut_edges)

        def over_x(x):
            if -MARGIN <= x < MARGIN:
                return m_lo
            if cx - MARGIN <= x < cx + MARGIN:
                return m_hi
            return 0.0

        def up(v):
            return pltpu.roll(v, 7, 0)

        def down(v):
            return pltpu.roll(v, 1, 0)

        sides = [(YO, 1, n_lo), (YO + cy - 8, -1, n_hi)]
        if reach == MARGIN:
            sides += [(YO - 8, -1, one), (YO + cy, 1, one)]
        for r0, d, weight in sides:
            edge = sub == (3 if d > 0 else 4)
            inner = sub == (2 if d > 0 else 5)

            def cross(fy, v):
                return fy * up(v) if d > 0 else down(fy * v)

            def e_of(x):
                return jnp.where(edge, B1 * (at(INV, x, r0, 8) * cross(at(FY, x, r0, 8), at(y0, x, r0, 8))), 0.0)

            prev, cur, f_prev = e_of(-reach - 1), e_of(-reach), at(FX, -reach - 1, r0, 8)
            for x in range(-reach, cx + reach):
                nxt, f = e_of(x + 1), at(FX, x, r0, 8)
                fy, fz, inv = at(FY, x, r0, 8), at(FZ, x, r0, 8), at(INV, x, r0, 8)
                times = 1.0 + over_x(x)
                flow = jnp.where(edge, cross(fy, at(y1, x, r0, 8)), 0.0)
                flow = flow + jnp.where(inner, cross(fy, cur), 0.0)
                flow = flow + (fz * pltpu.roll(cur, nz - 1, 1) + pltpu.roll(fz * cur, 1, 1))
                side = (1.0 + over_x(x) * over_x(x + 1)) * (f * nxt) if x + 1 != MARGIN and x + 1 != cx - MARGIN else f * nxt
                side = side + (
                    (1.0 + over_x(x) * over_x(x - 1)) * (f_prev * prev)
                    if x != MARGIN and x != cx - MARGIN else f_prev * prev
                )
                fix = times * (A2 * cur + B2 * (inv * flow)) + B2 * (inv * side)
                put(z, x, r0, at(z, x, r0, 8) - weight * fix)
                prev, cur, f_prev = cur, nxt, f

    zero = jnp.zeros((8, nz), jnp.float32)
    cut(Y0, Y1, Z0, MARGIN)

    def image0(r0, carry):
        def use(x, value, total):
            half = 0.5 * total
            put(Y0B, x, r0, (value - at(INV, x, r0) * half) * (1.0 / theta))
            if 0 <= x < cx:
                put(W0, x - XO, r0 - (YO - 8), at(DIAG, x, r0) * value - half)

        sweep(Z0, -3, cx + 3, r0, use)
        return carry

    strips(image0)
    precondition(Y0B, Y1, Z1, 1)

    def image1(t, carry):
        r0 = pl.multiple_of(YO + own_strip * t, 8)
        sums = list(carry)

        def use(x, value, total):
            w1 = at(DIAG, x, r0, own_strip) * value - 0.5 * total
            put(W1, x - XO, r0 - YO, w1)
            r, z0 = at(R, x, r0, own_strip), at(Z0, x, r0, own_strip)
            w0 = at(W0, x - XO, r0 - (YO - 8), own_strip)
            for q, (a, b) in enumerate(((r, z0), (z0, w0), (r, value), (w0, value), (z0, w1), (value, w1))):
                sums[q] = sums[q] + jnp.sum((a * b).reshape(own_strip // 8, 8, nz), axis=0)

        sweep(Z1, 0, cx, r0, use, own_strip)
        return tuple(sums)

    sums = lax.fori_loop(0, brick // own_strip, image1, (zero,) * 6)

    group_of = lax.broadcasted_iota(jnp.int32, (8, nz), 1) // 16
    mine = zero
    for q, acc in enumerate(sums):
        mine = jnp.where(sub == q, jnp.sum(acc, axis=0, keepdims=True), mine)
    for shift in (64, 32, 16):
        mine = mine + pltpu.roll(mine, shift, 1)
    part[0] = jnp.sum(jnp.where(sub == group_of, mine, 0.0), axis=0, keepdims=True)
    base = 0
    sent = []
    for s, dims in enumerate(STAGES):
        offs = offsets(dims)
        for n, off in enumerate(offs):
            pltpu.make_async_remote_copy(
                part.at[s], slots.at[base + n], ar_send.at[s], ar_recv.at[s],
                device_id=partner(gx, gy, dims, off), device_id_type=MESH,
            ).start()
        group = slots.at[pl.ds(base, len(offs))]
        both = pltpu.make_async_remote_copy(
            group, group, ar_send.at[s], ar_recv.at[s],
            device_id=partner(gx, gy, dims, offs[0]), device_id_type=MESH,
        )
        both.wait_recv()
        sent.append(both)
        part[s + 1] = part[s] + jnp.sum(slots[base : base + len(offs)], axis=0)
        base += len(offs)
    totals = jnp.where(sub == group_of, jnp.broadcast_to(part[len(STAGES)], (8, nz)), 0.0)
    totals = jnp.sum(totals, axis=1, keepdims=True)
    rz, zw, rz1, wz1, zw1, z1w1 = [totals[q : q + 1] for q in range(6)]
    step0 = rz / zw
    next_rz = rz - step0 * (rz1 + zw) + step0 * step0 * wz1
    grow = 1.0 + next_rz / rz
    curve = grow * grow * zw - grow * step0 * (zw1 + wz1) + step0 * step0 * z1w1
    step1 = next_rz / curve
    g0, g1 = step0 + step1 * grow, step1 * step0
    g0 = jnp.broadcast_to(g0, (brick, nz))
    g1 = jnp.broadcast_to(g1, (brick, nz))

    def finish(x, carry):
        z0, z1 = at(Z0, x, YO, brick), at(Z1, x, YO, brick)
        w0, w1 = at(W0, x - XO, 8, brick), at(W1, x - XO, 0, brick)
        sol[x] = g0 * z0 - g1 * z1
        res[x] = at(R, x, YO, brick) - g0 * w0 + g1 * w1
        return carry

    lax.fori_loop(0, cx, finish, 0)
    for both in sent:
        both.wait_send()
    for k, (dx, dy) in enumerate(NEAR):

        @pl.when(here(dx, dy))
        def _():
            for copy in halo_copies(k, dx, dy):
                copy.wait_send()


def shards(right_side, conductivity):
    cx, cy, nz = right_side.shape
    ext = pltpu.VMEM((cx + 2 * KW, cy + 2 * YO, nz), jnp.float32)
    dma = pltpu.SemaphoreType.DMA
    hbm = pl.BlockSpec(memory_space=pltpu.MemorySpace.HBM)
    out = jax.ShapeDtypeStruct((cx, cy, nz), jnp.float32)
    right_side, conductivity = (
        pltpu.with_memory_space_constraint(v, pltpu.MemorySpace.HBM) for v in (right_side, conductivity)
    )
    return pl.pallas_call(
        kernel,
        out_shape=(out, out),
        in_specs=[hbm, hbm],
        out_specs=(pl.BlockSpec(memory_space=pltpu.MemorySpace.VMEM),) * 2,
        scratch_shapes=[ext] * 12
        + [
            pltpu.VMEM((cx, cy + 16, nz), jnp.float32),
            pltpu.VMEM((cx, cy, nz), jnp.float32),
            pltpu.VMEM((2, SIDE * cx + 8, nz), jnp.float32),
            pltpu.VMEM((2, SIDE * cx + 16, nz), jnp.float32),
            pltpu.VMEM((4, CORNER_ROWS + 8, nz), jnp.float32),
            pltpu.VMEM((4, CORNER_ROWS + 16, nz), jnp.float32),
            pltpu.VMEM((len(STAGES) + 1, 1, nz), jnp.float32),
            pltpu.VMEM((N_SLOTS, 1, nz), jnp.float32),
            dma((2,)), dma((16,)), dma((16,)), dma((len(STAGES),)), dma((len(STAGES),)),
        ],
        compiler_params=pltpu.CompilerParams(
            collective_id=0, has_side_effects=True, vmem_limit_bytes=40 << 20
        ),
    )(right_side, conductivity)


def solution(mesh):
    spec = P("gx", "gy", None)
    return jax.shard_map(
        shards, mesh=mesh, in_specs=(spec, spec), out_specs=(spec, spec), check_vma=False
    )
```

```python
import itertools

import jax
import jax.numpy as jnp
from jax import lax
from jax.experimental import pallas as pl
from jax.experimental.pallas import tpu as pltpu
from jax.sharding import PartitionSpec as P

MESH = pl.DeviceIdType.MESH
MARGIN = 4
absorb = 0.05
theta = 1.05
delta = 0.95

sig = theta / delta
rho0 = 1.0 / sig
rho1 = 1.0 / (2.0 * sig - rho0)
rho2 = 1.0 / (2.0 * sig - rho1)
c1, c2 = rho1 * rho0, 2.0 * rho1 / delta
c3, c4 = rho2 * rho1, 2.0 * rho2 / delta
A1 = 1.0 + c1 + c2 * (theta - 1.0)
B1 = 0.5 * c2
A2 = 1.0 + c3 - c4
A0 = c4 * theta - c3
B2 = 0.5 * c4

KW, RW = 7, 6
GUARD = 8
YO = 16
XO = KW

SIZES = dict(c=2, x=4, y=4, z=8)
STAGES = (("c",), ("x", "y"), ("z",))
CORNERS = ((-1, -1), (-1, 1), (1, -1), (1, 1))
NEAR = CORNERS + ((0, -1), (0, 1), (-1, 0), (1, 0))


def offsets(dims):
    def hops(off):
        return sum(min(o, SIZES[d] - o) for d, o in zip(dims, off))

    every = itertools.product(*[range(SIZES[d]) for d in dims])
    return sorted((off for off in every if any(off)), key=hops, reverse=True)


N_SLOTS = sum(len(offsets(dims)) for dims in STAGES)


def partner(gx, gy, dims, off):
    me = dict(c=gx % 2, x=(gx // 2) % 4, y=gy % 4, z=gx // 8 + 4 * (gy // 4))
    for d, o in zip(dims, off):
        me[d] = (me[d] + o) % SIZES[d]
    return ((me["z"] % 4) * 8 + me["x"] * 2 + me["c"], (me["z"] // 4) * 4 + me["y"])


def triangle(start, width):
    out = []
    for d in range(1, width):
        out.append((d, start, width - d))
        start += width - d
    return out


K_CORNER = triangle(0, KW)
R_CORNER = triangle(sum(n for _, _, n in K_CORNER), RW)
CORNER_ROWS = 40
SIDE = KW + RW


def kernel(
    r_hbm, k_hbm, sol, res,
    K, R, INV, DIAG, FX, FY, FZ, Y0, Y1, Y0B, Z0, Z1, W0, W1, side_out, side_in, corner_out, corner_in, part, slots,
    load_sem, send_sem, recv_sem, ar_send, ar_recv,
):
    cx, cy, nz = r_hbm.shape
    n_gx, n_gy = lax.axis_size("gx"), lax.axis_size("gy")
    gx, gy = lax.axis_index("gx"), lax.axis_index("gy")
    full, brick = cy + 16, cy
    strip = 48 if full % 48 == 0 else 8
    own_strip = 64 if brick % 64 == 0 else 8

    def here(dx, dy):
        return (gx + dx >= 0) & (gx + dx < n_gx) & (gy + dy >= 0) & (gy + dy < n_gy)

    piece = cx // 4
    loads = [
        pltpu.make_async_copy(
            src.at[pl.ds(x, piece)], dst.at[pl.ds(XO + x, piece), pl.ds(YO, cy)], load_sem.at[n, x // piece]
        )
        for n, (src, dst) in enumerate(((k_hbm, K), (r_hbm, R)))
        for x in range(0, cx, piece)
    ]
    for load in loads:
        load.start()

    barrier = pltpu.get_barrier_semaphore()
    count = 0
    for dx, dy in NEAR:
        count = count + here(dx, dy).astype(jnp.int32)

        @pl.when(here(dx, dy))
        def _():
            pl.semaphore_signal(barrier, inc=1, device_id=(gx + dx, gy + dy), device_id_type=MESH)

    for dims in STAGES:
        for off in offsets(dims):
            pl.semaphore_signal(
                barrier, inc=1, device_id=partner(gx, gy, dims, off), device_id_type=MESH
            )
            count = count + 1

    for load in loads:
        load.wait()

    def pack(x, carry):
        for s, (k_row, r_row) in enumerate(((YO, YO), (YO + cy - KW, YO + cy - RW))):
            side_out[s, pl.ds(SIDE * x, 8)] = K[x + XO, pl.ds(k_row, 8)]
            side_out[s, pl.ds(SIDE * x + KW, 8)] = R[x + XO, pl.ds(r_row, 8)]
        return carry

    lax.fori_loop(0, cx, pack, 0)
    for c, (dx, dy) in enumerate(CORNERS):
        for ref, parts in ((K, K_CORNER), (R, R_CORNER)):
            for d, start, n in parts:
                x = XO + (cx - d if dx > 0 else d - 1)
                corner_out[c, pl.ds(start, 8)] = ref[x, pl.ds(YO + cy - n if dy > 0 else YO, 8)]

    pl.semaphore_wait(barrier, count)

    def halo_copies(k, dx, dy):
        if dx and dy:
            pairs = [(corner_out.at[k, pl.ds(0, CORNER_ROWS)], corner_in.at[k, pl.ds(8, CORNER_ROWS)])]
        elif dy:
            s = (dy + 1) // 2
            pairs = [(side_out.at[s, pl.ds(0, SIDE * cx)], side_in.at[s, pl.ds(8, SIDE * cx)])]
        else:
            pairs = []
            for src, dst, width in ((k_hbm, K, KW), (r_hbm, R, RW)):
                sx = cx - width if dx > 0 else 0
                tx = XO - width if dx > 0 else XO + cx
                pairs.append((src.at[pl.ds(sx, width)], dst.at[pl.ds(tx, width), pl.ds(YO, cy)]))
        return [
            pltpu.make_async_remote_copy(
                src, dst, send_sem.at[2 * k + n], recv_sem.at[2 * k + n],
                device_id=(gx + dx, gy + dy), device_id_type=MESH,
            )
            for n, (src, dst) in enumerate(pairs)
        ]

    def send(along_x):
        for k, (dx, dy) in enumerate(NEAR):
            if along_x == (dy == 0):

                @pl.when(here(dx, dy))
                def _():
                    for copy in halo_copies(k, dx, dy):
                        copy.start()

    send(False)
    send(True)

    sub = lax.broadcasted_iota(jnp.int32, (8, nz), 0)

    def line_of(h):
        return lax.broadcasted_iota(jnp.int32, (h, nz), 0)

    one = jnp.float32(1.0)
    m_lo = jnp.where(gx > 0, one, 0.0)
    m_hi = jnp.where(gx < n_gx - 1, one, 0.0)
    has_lo, has_hi = gy > 0, gy < n_gy - 1
    n_lo = jnp.where(has_lo, one, 0.0)
    n_hi = jnp.where(has_hi, one, 0.0)

    def at(ref, x, row, h=strip):
        return ref[x + XO, pl.ds(row, h), :]

    def put(ref, x, row, value):
        ref[x + XO, pl.ds(row, value.shape[0]), :] = value

    def strip_row(t):
        return pl.multiple_of(YO - 8 + strip * t, 8)

    def strips(body):
        lax.fori_loop(0, full // strip, lambda t, c: body(strip_row(t), c), 0)

    core, tall = cy - 16, 64 if cy % 64 == 0 else 8
    core_strip = 56 if core % 56 == 0 else 8

    def inside(stage, m):
        def body(t, carry):
            stage(pl.multiple_of(YO + tall * t, 8), m, cx - m, tall)
            return carry

        lax.fori_loop(0, cy // tall, body, 0)

    def around(stage, m, reach):
        def sides(t, carry):
            r0 = pl.multiple_of(YO + 8 + core_strip * t, 8)
            stage(r0, -reach, m, core_strip)
            stage(r0, cx - m, cx + reach, core_strip)
            return carry

        def ends(t, carry):
            stage(pl.multiple_of(YO - 8 + cy * t, 8), -reach, cx + reach, 16)
            return carry

        lax.fori_loop(0, core // core_strip, sides, 0)
        lax.fori_loop(0, 2, ends, 0)

    def coefficients(r0, lo, hi, h):
        lane = lax.broadcasted_iota(jnp.int32, (h, nz), 1)
        first_lane, last_lane = lane == 0, lane == nz - 1
        low, mid = at(K, lo - 1, r0, h), at(K, lo, r0, h)
        for x in range(lo, hi):
            high = at(K, x + 1, r0, h)
            up, down = at(K, x, r0 + 1, h), at(K, x, r0 - 1, h)
            right = jnp.where(last_lane, mid, pltpu.roll(mid, nz - 1, 1))
            left = jnp.where(first_lane, mid, pltpu.roll(mid, 1, 1))
            diag = (absorb + 3.0 * mid) + 0.5 * ((low + high) + (up + down) + (left + right))
            inv = 1.0 / diag
            if 0 <= x < cx:
                put(DIAG, x, r0, diag)
            put(INV, x, r0, inv)
            put(FX, x, r0, mid + high)
            put(FY, x, r0, mid + up)
            put(FZ, x, r0, jnp.where(last_lane, 0.0, mid + right))
            low, mid = mid, high

    def start(r0, lo, hi, h):
        for x in range(lo, hi):
            put(Y0, x, r0, at(R, x, r0, h) * (at(INV, x, r0, h) * (1.0 / theta)))

    def sweep(src, lo, hi, r0, use, h=strip):
        prev, cur, f_prev = at(src, lo - 1, r0, h), at(src, lo, r0, h), at(FX, lo - 1, r0, h)
        for x in range(lo, hi):
            nxt, f = at(src, x + 1, r0, h), at(FX, x, r0, h)
            fz = at(FZ, x, r0, h)
            total = f * nxt + f_prev * prev
            total = total + (
                at(FY, x, r0, h) * at(src, x, r0 + 1, h) + at(FY, x, r0 - 1, h) * at(src, x, r0 - 1, h)
            )
            total = total + (fz * pltpu.roll(cur, nz - 1, 1) + pltpu.roll(fz * cur, 1, 1))
            use(x, cur, total)
            prev, cur, f_prev = cur, nxt, f

    def in_overlap(row):
        return ((row >= -MARGIN) & (row < MARGIN) & has_lo) | (
            (row >= cy - MARGIN) & (row < cy + MARGIN) & has_hi
        )

    def counts(r0, h):
        row = line_of(h) + (r0 - YO)
        over = jnp.where(in_overlap(row), one, 0.0)
        return row, over, 1.0 + over

    def first(y0, y1):
        def stage(r0, lo, hi, h):
            def use(x, value, total):
                put(y1, x, r0, A1 * value + B1 * (at(INV, x, r0, h) * total))

            sweep(y0, lo, hi, r0, use, h)

        return stage

    def second(y0, y1, z):
        def stage(r0, lo, hi, h):
            _, _, times = counts(r0, h)

            def use(x, value, total):
                y2 = A2 * value + A0 * at(y0, x, r0, h) + B2 * (at(INV, x, r0, h) * total)
                weight = 1.0 + m_lo if x < MARGIN else (1.0 + m_hi if x >= cx - MARGIN else one)
                put(z, x, r0, (weight * times) * y2)

            sweep(y1, lo, hi, r0, use, h)

        return stage

    inside(coefficients, 1)
    inside(start, 1)
    inside(first(Y0, Y1), 2)
    inside(second(Y0, Y1, Z0), 3)

    rows = cy + 16
    flat = lambda n: jnp.zeros((n, nz), jnp.float32)

    @pl.when(gx == 0)
    def _():
        for x in range(XO):
            K[x, pl.ds(YO - 8, rows)] = flat(rows)
            R[x, pl.ds(YO - 8, rows)] = flat(rows)

    @pl.when(gx == n_gx - 1)
    def _():
        for x in range(XO + cx, XO + cx + KW):
            K[x, pl.ds(YO - 8, rows)] = flat(rows)
            R[x, pl.ds(YO - 8, rows)] = flat(rows)

    for k, (dx, dy) in enumerate(NEAR):

        @pl.when(here(-dx, -dy))
        def _():
            for copy in halo_copies(k, dx, dy)[: 1 if dy == 0 else 2]:
                copy.wait_recv()

    for s, (dy, k_off, r_off) in enumerate(((-1, 8, 8 + KW), (1, 8 + KW - 8, 8 + SIDE - 8))):

        @pl.when(here(0, -dy))
        def _():
            row = YO - 8 if dy > 0 else YO + cy

            def unpack(x, carry):
                K[x + XO, pl.ds(row, 8)] = side_in[s, pl.ds(SIDE * x + k_off, 8)]
                R[x + XO, pl.ds(row, 8)] = side_in[s, pl.ds(SIDE * x + r_off, 8)]
                return carry

            lax.fori_loop(0, cx, unpack, 0)

    for c, (dx, dy) in enumerate(CORNERS):

        @pl.when(here(-dx, -dy))
        def _():
            row = YO - 8 if dy > 0 else YO + cy
            for ref, parts in ((K, K_CORNER), (R, R_CORNER)):
                for d, start, n in parts:
                    x = XO + (-d if dx > 0 else cx + d - 1)
                    ref[x, pl.ds(row, 8)] = corner_in[c, pl.ds(start + (n if dy > 0 else 8), 8)]

    @pl.when(gx == 0)
    def _():
        K[XO - 1, pl.ds(YO - 8, rows)] = K[XO, pl.ds(YO - 8, rows)]

    @pl.when(gx == n_gx - 1)
    def _():
        K[XO + cx, pl.ds(YO - 8, rows)] = K[XO + cx - 1, pl.ds(YO - 8, rows)]

    n_layers = cx + 2 * KW

    @pl.when(gy == 0)
    def _():
        for x in range(n_layers):
            K[x, pl.ds(YO - 8, 8)] = jnp.broadcast_to(K[x, pl.ds(YO, 1)], (8, nz))
            R[x, pl.ds(YO - 8, 8)] = flat(8)

    @pl.when(gy == n_gy - 1)
    def _():
        for x in range(n_layers):
            K[x, pl.ds(YO + cy, 8)] = jnp.broadcast_to(K[x, pl.ds(YO + cy - 1, 1)], (8, nz))
            R[x, pl.ds(YO + cy, 8)] = flat(8)

    around(coefficients, 1, RW)

    for k, (dx, dy) in enumerate(NEAR):
        if dy == 0:

            @pl.when(here(-dx, -dy))
            def _():
                halo_copies(k, dx, dy)[1].wait_recv()

    around(start, 1, RW)

    @pl.when(gx == 0)
    def _():
        FX[XO - 1, pl.ds(YO - 8, rows)] = flat(rows)

    @pl.when(gx == n_gx - 1)
    def _():
        FX[XO + cx - 1, pl.ds(YO - 8, rows)] = flat(rows)

    @pl.when(gy == 0)
    def _():
        for x in range(n_layers):
            FY[x, pl.ds(YO - 1, 1)] = flat(1)

    @pl.when(gy == n_gy - 1)
    def _():
        for x in range(n_layers):
            FY[x, pl.ds(YO + cy - 1, 1)] = flat(1)

    around(first(Y0, Y1), 2, MARGIN + 1)
    around(second(Y0, Y1, Z0), 3, MARGIN)

    def precondition(y0, y1, z, reach):
        strips(lambda r0, c: (first(y0, y1)(r0, -reach - 1, cx + reach + 1, strip), c)[1])
        strips(lambda r0, c: (second(y0, y1, z)(r0, -reach, cx + reach, strip), c)[1])
        cut(y0, y1, z, reach)

    def cut(y0, y1, z, reach):
        edges = [(MARGIN - 1, 1, m_lo), (cx - MARGIN, -1, m_hi)]
        if reach == MARGIN:
            edges += [(-MARGIN, -1, one), (cx + MARGIN - 1, 1, one)]

        def cut_edges(r0, carry):
            row, over, times = counts(r0, strip)
            pair_up = 1.0 + over * jnp.where(in_overlap(row + 1), one, 0.0)
            pair_down = 1.0 + over * jnp.where(in_overlap(row - 1), one, 0.0)
            for a, d, weight in edges:
                def face(row0):
                    return at(FX, a if d > 0 else a - 1, row0)

                def e_at(row0):
                    return B1 * (at(INV, a, row0) * (face(row0) * at(y0, a + d, row0)))

                e, e_up, e_down = e_at(r0), e_at(r0 + 1), e_at(r0 - 1)
                fz, inv = at(FZ, a, r0), at(INV, a, r0)
                flow = face(r0) * at(y1, a + d, r0) + (
                    fz * pltpu.roll(e, nz - 1, 1) + pltpu.roll(fz * e, 1, 1)
                )
                side = at(FY, a, r0) * (pair_up * e_up) + at(FY, a, r0 - 1) * (pair_down * e_down)
                fix = times * (A2 * e + B2 * (inv * flow)) + B2 * (inv * side)
                put(z, a, r0, at(z, a, r0) - weight * fix)
                inner = at(FX, a - 1 if d > 0 else a, r0)
                fix = (weight * B2) * (times * (at(INV, a - d, r0) * (inner * e)))
                put(z, a - d, r0, at(z, a - d, r0) - fix)
            return carry

        strips(cut_edges)

        def over_x(x):
            if -MARGIN <= x < MARGIN:
                return m_lo
            if cx - MARGIN <= x < cx + MARGIN:
                return m_hi
            return 0.0

        def up(v):
            return pltpu.roll(v, 7, 0)

        def down(v):
            return pltpu.roll(v, 1, 0)

        sides = [(YO, 1, n_lo), (YO + cy - 8, -1, n_hi)]
        if reach == MARGIN:
            sides += [(YO - 8, -1, one), (YO + cy, 1, one)]
        for r0, d, weight in sides:
            edge = sub == (3 if d > 0 else 4)
            inner = sub == (2 if d > 0 else 5)

            def cross(fy, v):
                return fy * up(v) if d > 0 else down(fy * v)

            def e_of(x):
                return jnp.where(edge, B1 * (at(INV, x, r0, 8) * cross(at(FY, x, r0, 8), at(y0, x, r0, 8))), 0.0)

            prev, cur, f_prev = e_of(-reach - 1), e_of(-reach), at(FX, -reach - 1, r0, 8)
            for x in range(-reach, cx + reach):
                nxt, f = e_of(x + 1), at(FX, x, r0, 8)
                fy, fz, inv = at(FY, x, r0, 8), at(FZ, x, r0, 8), at(INV, x, r0, 8)
                times = 1.0 + over_x(x)
                flow = jnp.where(edge, cross(fy, at(y1, x, r0, 8)), 0.0)
                flow = flow + jnp.where(inner, cross(fy, cur), 0.0)
                flow = flow + (fz * pltpu.roll(cur, nz - 1, 1) + pltpu.roll(fz * cur, 1, 1))
                side = (1.0 + over_x(x) * over_x(x + 1)) * (f * nxt) if x + 1 != MARGIN and x + 1 != cx - MARGIN else f * nxt
                side = side + (
                    (1.0 + over_x(x) * over_x(x - 1)) * (f_prev * prev)
                    if x != MARGIN and x != cx - MARGIN else f_prev * prev
                )
                fix = times * (A2 * cur + B2 * (inv * flow)) + B2 * (inv * side)
                put(z, x, r0, at(z, x, r0, 8) - weight * fix)
                prev, cur, f_prev = cur, nxt, f

    zero = jnp.zeros((8, nz), jnp.float32)
    cut(Y0, Y1, Z0, MARGIN)

    def image0(r0, carry):
        def use(x, value, total):
            half = 0.5 * total
            put(Y0B, x, r0, (value - at(INV, x, r0) * half) * (1.0 / theta))
            if 0 <= x < cx:
                put(W0, x - XO, r0 - (YO - 8), at(DIAG, x, r0) * value - half)

        sweep(Z0, -3, cx + 3, r0, use)
        return carry

    strips(image0)
    precondition(Y0B, Y1, Z1, 1)

    def image1(t, carry):
        r0 = pl.multiple_of(YO + own_strip * t, 8)
        sums = list(carry)

        def use(x, value, total):
            w1 = at(DIAG, x, r0, own_strip) * value - 0.5 * total
            put(W1, x - XO, r0 - YO, w1)
            r, z0 = at(R, x, r0, own_strip), at(Z0, x, r0, own_strip)
            w0 = at(W0, x - XO, r0 - (YO - 8), own_strip)
            for q, (a, b) in enumerate(((r, z0), (z0, w0), (r, value), (w0, value), (z0, w1), (value, w1))):
                sums[q] = sums[q] + jnp.sum((a * b).reshape(own_strip // 8, 8, nz), axis=0)

        sweep(Z1, 0, cx, r0, use, own_strip)
        return tuple(sums)

    sums = lax.fori_loop(0, brick // own_strip, image1, (zero,) * 6)

    group_of = lax.broadcasted_iota(jnp.int32, (8, nz), 1) // 16
    mine = zero
    for q, acc in enumerate(sums):
        mine = jnp.where(sub == q, jnp.sum(acc, axis=0, keepdims=True), mine)
    for shift in (64, 32, 16):
        mine = mine + pltpu.roll(mine, shift, 1)
    part[0] = jnp.sum(jnp.where(sub == group_of, mine, 0.0), axis=0, keepdims=True)
    base = 0
    sent = []
    for s, dims in enumerate(STAGES):
        offs = offsets(dims)
        for n, off in enumerate(offs):
            pltpu.make_async_remote_copy(
                part.at[s], slots.at[base + n], ar_send.at[s], ar_recv.at[s],
                device_id=partner(gx, gy, dims, off), device_id_type=MESH,
            ).start()
        group = slots.at[pl.ds(base, len(offs))]
        both = pltpu.make_async_remote_copy(
            group, group, ar_send.at[s], ar_recv.at[s],
            device_id=partner(gx, gy, dims, offs[0]), device_id_type=MESH,
        )
        both.wait_recv()
        sent.append(both)
        part[s + 1] = part[s] + jnp.sum(slots[base : base + len(offs)], axis=0)
        base += len(offs)
    totals = jnp.where(sub == group_of, jnp.broadcast_to(part[len(STAGES)], (8, nz)), 0.0)
    totals = jnp.sum(totals, axis=1, keepdims=True)
    rz, zw, rz1, wz1, zw1, z1w1 = [totals[q : q + 1] for q in range(6)]
    step0 = rz / zw
    next_rz = rz - step0 * (rz1 + zw) + step0 * step0 * wz1
    grow = 1.0 + next_rz / rz
    curve = grow * grow * zw - grow * step0 * (zw1 + wz1) + step0 * step0 * z1w1
    step1 = next_rz / curve
    g0, g1 = step0 + step1 * grow, step1 * step0
    g0 = jnp.broadcast_to(g0, (brick, nz))
    g1 = jnp.broadcast_to(g1, (brick, nz))

    def finish(x, carry):
        z0, z1 = at(Z0, x, YO, brick), at(Z1, x, YO, brick)
        w0, w1 = at(W0, x - XO, 8, brick), at(W1, x - XO, 0, brick)
        sol[x] = g0 * z0 - g1 * z1
        res[x] = at(R, x, YO, brick) - g0 * w0 + g1 * w1
        return carry

    lax.fori_loop(0, cx, finish, 0)
    for both in sent:
        both.wait_send()
    for k, (dx, dy) in enumerate(NEAR):

        @pl.when(here(dx, dy))
        def _():
            for copy in halo_copies(k, dx, dy):
                copy.wait_send()


def shards(right_side, conductivity):
    cx, cy, nz = right_side.shape
    ext = pltpu.VMEM((cx + 2 * KW, cy + 2 * YO, nz), jnp.float32)
    dma = pltpu.SemaphoreType.DMA
    hbm = pl.BlockSpec(memory_space=pltpu.MemorySpace.HBM)
    out = jax.ShapeDtypeStruct((cx, cy, nz), jnp.float32)
    right_side, conductivity = (
        pltpu.with_memory_space_constraint(v, pltpu.MemorySpace.HBM) for v in (right_side, conductivity)
    )
    return pl.pallas_call(
        kernel,
        out_shape=(out, out),
        in_specs=[hbm, hbm],
        out_specs=(pl.BlockSpec(memory_space=pltpu.MemorySpace.VMEM),) * 2,
        scratch_shapes=[ext] * 12
        + [
            pltpu.VMEM((cx, cy + 16, nz), jnp.float32),
            pltpu.VMEM((cx, cy, nz), jnp.float32),
            pltpu.VMEM((2, SIDE * cx + 8, nz), jnp.float32),
            pltpu.VMEM((2, SIDE * cx + 16, nz), jnp.float32),
            pltpu.VMEM((4, CORNER_ROWS + 8, nz), jnp.float32),
            pltpu.VMEM((4, CORNER_ROWS + 16, nz), jnp.float32),
            pltpu.VMEM((len(STAGES) + 1, 1, nz), jnp.float32),
            pltpu.VMEM((N_SLOTS, 1, nz), jnp.float32),
            dma((2, 4)), dma((16,)), dma((16,)), dma((len(STAGES),)), dma((len(STAGES),)),
        ],
        compiler_params=pltpu.CompilerParams(
            collective_id=0, has_side_effects=True, vmem_limit_bytes=40 << 20
        ),
    )(right_side, conductivity)


def solution(mesh):
    spec = P("gx", "gy", None)
    return jax.shard_map(
        shards, mesh=mesh, in_specs=(spec, spec), out_specs=(spec, spec), check_vma=False
    )
```

```python
import itertools

import jax
import jax.numpy as jnp
from jax import lax
from jax.experimental import pallas as pl
from jax.experimental.pallas import tpu as pltpu
from jax.sharding import PartitionSpec as P

MESH = pl.DeviceIdType.MESH
MARGIN = 4
absorb = 0.05
theta = 1.05
delta = 0.95

sig = theta / delta
rho0 = 1.0 / sig
rho1 = 1.0 / (2.0 * sig - rho0)
rho2 = 1.0 / (2.0 * sig - rho1)
c1, c2 = rho1 * rho0, 2.0 * rho1 / delta
c3, c4 = rho2 * rho1, 2.0 * rho2 / delta
A1 = 1.0 + c1 + c2 * (theta - 1.0)
B1 = 0.5 * c2
A2 = 1.0 + c3 - c4
A0 = c4 * theta - c3
B2 = 0.5 * c4

KW, RW = 7, 6
GUARD = 8
YO = 16
XO = KW

SIZES = dict(c=2, x=4, y=4, z=8)
STAGES = (("c",), ("x", "y"), ("z",))
CORNERS = ((-1, -1), (-1, 1), (1, -1), (1, 1))
NEAR = CORNERS + ((0, -1), (0, 1), (-1, 0), (1, 0))


def offsets(dims):
    def hops(off):
        return sum(min(o, SIZES[d] - o) for d, o in zip(dims, off))

    every = itertools.product(*[range(SIZES[d]) for d in dims])
    return sorted((off for off in every if any(off)), key=hops, reverse=True)


N_SLOTS = sum(len(offsets(dims)) for dims in STAGES)


def partner(gx, gy, dims, off):
    me = dict(c=gx % 2, x=(gx // 2) % 4, y=gy % 4, z=gx // 8 + 4 * (gy // 4))
    for d, o in zip(dims, off):
        me[d] = (me[d] + o) % SIZES[d]
    return ((me["z"] % 4) * 8 + me["x"] * 2 + me["c"], (me["z"] // 4) * 4 + me["y"])


def triangle(start, width):
    out = []
    for d in range(1, width):
        out.append((d, start, width - d))
        start += width - d
    return out


K_CORNER = triangle(0, KW)
R_CORNER = triangle(sum(n for _, _, n in K_CORNER), RW)
CORNER_ROWS = 40
SIDE = KW + RW


def kernel(
    r_hbm, k_hbm, sol, res,
    K, R, INV, DIAG, FX, FY, FZ, Y0, Y1, Y0B, Z0, Z1, W0, W1, side_out, side_in, corner_out, corner_in, part, slots,
    load_sem, send_sem, recv_sem, ar_send, ar_recv,
):
    cx, cy, nz = r_hbm.shape
    n_gx, n_gy = lax.axis_size("gx"), lax.axis_size("gy")
    gx, gy = lax.axis_index("gx"), lax.axis_index("gy")
    full, brick = cy + 16, cy
    strip = 48 if full % 48 == 0 else 8
    own_strip = 64 if brick % 64 == 0 else 8

    def here(dx, dy):
        return (gx + dx >= 0) & (gx + dx < n_gx) & (gy + dy >= 0) & (gy + dy < n_gy)

    piece = cx // 4
    loads = [
        pltpu.make_async_copy(
            src.at[pl.ds(x, piece)], dst.at[pl.ds(XO + x, piece), pl.ds(YO, cy)], load_sem.at[n, x // piece]
        )
        for n, (src, dst) in enumerate(((k_hbm, K), (r_hbm, R)))
        for x in range(0, cx, piece)
    ]
    for load in loads:
        load.start()

    barrier = pltpu.get_barrier_semaphore()
    count = 0
    for dx, dy in NEAR:
        count = count + here(dx, dy).astype(jnp.int32)

        @pl.when(here(dx, dy))
        def _():
            pl.semaphore_signal(barrier, inc=1, device_id=(gx + dx, gy + dy), device_id_type=MESH)

    for dims in STAGES:
        for off in offsets(dims):
            pl.semaphore_signal(
                barrier, inc=1, device_id=partner(gx, gy, dims, off), device_id_type=MESH
            )
            count = count + 1

    for load in loads:
        load.wait()

    def pack(x, carry):
        for s, (k_row, r_row) in enumerate(((YO, YO), (YO + cy - KW, YO + cy - RW))):
            side_out[s, pl.ds(SIDE * x, 8)] = K[x + XO, pl.ds(k_row, 8)]
            side_out[s, pl.ds(SIDE * x + KW, 8)] = R[x + XO, pl.ds(r_row, 8)]
        return carry

    lax.fori_loop(0, cx, pack, 0)
    for c, (dx, dy) in enumerate(CORNERS):
        for ref, parts in ((K, K_CORNER), (R, R_CORNER)):
            for d, start, n in parts:
                x = XO + (cx - d if dx > 0 else d - 1)
                corner_out[c, pl.ds(start, 8)] = ref[x, pl.ds(YO + cy - n if dy > 0 else YO, 8)]

    pl.semaphore_wait(barrier, count)

    def halo_copies(k, dx, dy):
        if dx and dy:
            pairs = [(corner_out.at[k, pl.ds(0, CORNER_ROWS)], corner_in.at[k, pl.ds(8, CORNER_ROWS)])]
        elif dy:
            s = (dy + 1) // 2
            pairs = [(side_out.at[s, pl.ds(0, SIDE * cx)], side_in.at[s, pl.ds(8, SIDE * cx)])]
        else:
            pairs = []
            for src, dst, width in ((k_hbm, K, KW), (r_hbm, R, RW)):
                sx = cx - width if dx > 0 else 0
                tx = XO - width if dx > 0 else XO + cx
                pairs.append((src.at[pl.ds(sx, width)], dst.at[pl.ds(tx, width), pl.ds(YO, cy)]))
        return [
            pltpu.make_async_remote_copy(
                src, dst, send_sem.at[2 * k + n], recv_sem.at[2 * k + n],
                device_id=(gx + dx, gy + dy), device_id_type=MESH,
            )
            for n, (src, dst) in enumerate(pairs)
        ]

    def send(along_x, which):
        for k, (dx, dy) in enumerate(NEAR):
            if along_x == (dy == 0):

                @pl.when(here(dx, dy))
                def _():
                    halo_copies(k, dx, dy)[which].start()

    send(False, 0)
    send(True, 0)
    send(True, 1)

    sub = lax.broadcasted_iota(jnp.int32, (8, nz), 0)

    def line_of(h):
        return lax.broadcasted_iota(jnp.int32, (h, nz), 0)

    one = jnp.float32(1.0)
    m_lo = jnp.where(gx > 0, one, 0.0)
    m_hi = jnp.where(gx < n_gx - 1, one, 0.0)
    has_lo, has_hi = gy > 0, gy < n_gy - 1
    n_lo = jnp.where(has_lo, one, 0.0)
    n_hi = jnp.where(has_hi, one, 0.0)

    def at(ref, x, row, h=strip):
        return ref[x + XO, pl.ds(row, h), :]

    def put(ref, x, row, value):
        ref[x + XO, pl.ds(row, value.shape[0]), :] = value

    def strip_row(t):
        return pl.multiple_of(YO - 8 + strip * t, 8)

    def strips(body):
        lax.fori_loop(0, full // strip, lambda t, c: body(strip_row(t), c), 0)

    tall = 64 if cy % 64 == 0 else 8

    def inside(stage, m):
        def body(t, carry):
            stage(pl.multiple_of(YO + tall * t, 8), m, cx - m, tall)
            return carry

        lax.fori_loop(0, cy // tall, body, 0)

    def ends(stage, m):
        def body(t, carry):
            stage(pl.multiple_of(YO - 8 + cy * t, 8), m, cx - m, 16)
            return carry

        lax.fori_loop(0, 2, body, 0)

    def sides(stage, m, reach):
        def body(r0, carry):
            stage(r0, -reach, m, strip)
            stage(r0, cx - m, cx + reach, strip)
            return carry

        strips(body)

    def coefficients(r0, lo, hi, h):
        lane = lax.broadcasted_iota(jnp.int32, (h, nz), 1)
        first_lane, last_lane = lane == 0, lane == nz - 1
        low, mid = at(K, lo - 1, r0, h), at(K, lo, r0, h)
        for x in range(lo, hi):
            high = at(K, x + 1, r0, h)
            up, down = at(K, x, r0 + 1, h), at(K, x, r0 - 1, h)
            right = jnp.where(last_lane, mid, pltpu.roll(mid, nz - 1, 1))
            left = jnp.where(first_lane, mid, pltpu.roll(mid, 1, 1))
            diag = (absorb + 3.0 * mid) + 0.5 * ((low + high) + (up + down) + (left + right))
            inv = 1.0 / diag
            if 0 <= x < cx:
                put(DIAG, x, r0, diag)
            put(INV, x, r0, inv)
            put(FX, x, r0, mid + high)
            put(FY, x, r0, mid + up)
            put(FZ, x, r0, jnp.where(last_lane, 0.0, mid + right))
            low, mid = mid, high

    def start(r0, lo, hi, h):
        for x in range(lo, hi):
            put(Y0, x, r0, at(R, x, r0, h) * (at(INV, x, r0, h) * (1.0 / theta)))

    def sweep(src, lo, hi, r0, use, h=strip):
        prev, cur, f_prev = at(src, lo - 1, r0, h), at(src, lo, r0, h), at(FX, lo - 1, r0, h)
        for x in range(lo, hi):
            nxt, f = at(src, x + 1, r0, h), at(FX, x, r0, h)
            fz = at(FZ, x, r0, h)
            total = f * nxt + f_prev * prev
            total = total + (
                at(FY, x, r0, h) * at(src, x, r0 + 1, h) + at(FY, x, r0 - 1, h) * at(src, x, r0 - 1, h)
            )
            total = total + (fz * pltpu.roll(cur, nz - 1, 1) + pltpu.roll(fz * cur, 1, 1))
            use(x, cur, total)
            prev, cur, f_prev = cur, nxt, f

    def in_overlap(row):
        return ((row >= -MARGIN) & (row < MARGIN) & has_lo) | (
            (row >= cy - MARGIN) & (row < cy + MARGIN) & has_hi
        )

    def counts(r0, h):
        row = line_of(h) + (r0 - YO)
        over = jnp.where(in_overlap(row), one, 0.0)
        return row, over, 1.0 + over

    def first(y0, y1):
        def stage(r0, lo, hi, h):
            def use(x, value, total):
                put(y1, x, r0, A1 * value + B1 * (at(INV, x, r0, h) * total))

            sweep(y0, lo, hi, r0, use, h)

        return stage

    def second(y0, y1, z):
        def stage(r0, lo, hi, h):
            _, _, times = counts(r0, h)

            def use(x, value, total):
                y2 = A2 * value + A0 * at(y0, x, r0, h) + B2 * (at(INV, x, r0, h) * total)
                weight = 1.0 + m_lo if x < MARGIN else (1.0 + m_hi if x >= cx - MARGIN else one)
                put(z, x, r0, (weight * times) * y2)

            sweep(y1, lo, hi, r0, use, h)

        return stage

    inside(coefficients, 1)
    inside(start, 1)
    inside(first(Y0, Y1), 2)
    inside(second(Y0, Y1, Z0), 3)

    rows = cy + 16
    flat = lambda n: jnp.zeros((n, nz), jnp.float32)

    @pl.when(gx == 0)
    def _():
        for x in range(XO):
            K[x, pl.ds(YO - 8, rows)] = flat(rows)
            R[x, pl.ds(YO - 8, rows)] = flat(rows)

    @pl.when(gx == n_gx - 1)
    def _():
        for x in range(XO + cx, XO + cx + KW):
            K[x, pl.ds(YO - 8, rows)] = flat(rows)
            R[x, pl.ds(YO - 8, rows)] = flat(rows)


    def receive(along_x, which):
        for k, (dx, dy) in enumerate(NEAR):
            if along_x == (dy == 0):

                @pl.when(here(-dx, -dy))
                def _():
                    halo_copies(k, dx, dy)[which].wait_recv()

    receive(False, 0)

    for s, (dy, k_off, r_off) in enumerate(((-1, 8, 8 + KW), (1, 8 + KW - 8, 8 + SIDE - 8))):

        @pl.when(here(0, -dy))
        def _():
            row = YO - 8 if dy > 0 else YO + cy

            def unpack(x, carry):
                K[x + XO, pl.ds(row, 8)] = side_in[s, pl.ds(SIDE * x + k_off, 8)]
                R[x + XO, pl.ds(row, 8)] = side_in[s, pl.ds(SIDE * x + r_off, 8)]
                return carry

            lax.fori_loop(0, cx, unpack, 0)

    for c, (dx, dy) in enumerate(CORNERS):

        @pl.when(here(-dx, -dy))
        def _():
            row = YO - 8 if dy > 0 else YO + cy
            for ref, parts in ((K, K_CORNER), (R, R_CORNER)):
                for d, start, n in parts:
                    x = XO + (-d if dx > 0 else cx + d - 1)
                    ref[x, pl.ds(row, 8)] = corner_in[c, pl.ds(start + (n if dy > 0 else 8), 8)]

    own_layers = tuple(range(XO, XO + cx))
    halo_layers = tuple(range(XO)) + tuple(range(XO + cx, cx + 2 * KW))

    def mirror(layers):
        @pl.when(gy == 0)
        def _():
            for x in layers:
                K[x, pl.ds(YO - 8, 8)] = jnp.broadcast_to(K[x, pl.ds(YO, 1)], (8, nz))
                R[x, pl.ds(YO - 8, 8)] = flat(8)

        @pl.when(gy == n_gy - 1)
        def _():
            for x in layers:
                K[x, pl.ds(YO + cy, 8)] = jnp.broadcast_to(K[x, pl.ds(YO + cy - 1, 1)], (8, nz))
                R[x, pl.ds(YO + cy, 8)] = flat(8)

    def cut_faces(layers):
        @pl.when(gy == 0)
        def _():
            for x in layers:
                FY[x, pl.ds(YO - 1, 1)] = flat(1)

        @pl.when(gy == n_gy - 1)
        def _():
            for x in layers:
                FY[x, pl.ds(YO + cy - 1, 1)] = flat(1)

    mirror(own_layers)
    ends(coefficients, 1)
    ends(start, 1)
    cut_faces(own_layers)
    ends(first(Y0, Y1), 2)
    ends(second(Y0, Y1, Z0), 3)

    receive(True, 0)

    @pl.when(gx == 0)
    def _():
        K[XO - 1, pl.ds(YO - 8, rows)] = K[XO, pl.ds(YO - 8, rows)]

    @pl.when(gx == n_gx - 1)
    def _():
        K[XO + cx, pl.ds(YO - 8, rows)] = K[XO + cx - 1, pl.ds(YO - 8, rows)]

    mirror(halo_layers)
    sides(coefficients, 1, RW)

    receive(True, 1)
    sides(start, 1, RW)

    @pl.when(gx == 0)
    def _():
        FX[XO - 1, pl.ds(YO - 8, rows)] = flat(rows)

    @pl.when(gx == n_gx - 1)
    def _():
        FX[XO + cx - 1, pl.ds(YO - 8, rows)] = flat(rows)

    cut_faces(halo_layers + (XO, XO + cx - 1))
    sides(first(Y0, Y1), 2, MARGIN + 1)
    sides(second(Y0, Y1, Z0), 3, MARGIN)

    def precondition(y0, y1, z, reach):
        strips(lambda r0, c: (first(y0, y1)(r0, -reach - 1, cx + reach + 1, strip), c)[1])
        strips(lambda r0, c: (second(y0, y1, z)(r0, -reach, cx + reach, strip), c)[1])
        cut(y0, y1, z, reach)

    def cut(y0, y1, z, reach):
        edges = [(MARGIN - 1, 1, m_lo), (cx - MARGIN, -1, m_hi)]
        if reach == MARGIN:
            edges += [(-MARGIN, -1, one), (cx + MARGIN - 1, 1, one)]

        def cut_edges(r0, carry):
            row, over, times = counts(r0, strip)
            pair_up = 1.0 + over * jnp.where(in_overlap(row + 1), one, 0.0)
            pair_down = 1.0 + over * jnp.where(in_overlap(row - 1), one, 0.0)
            for a, d, weight in edges:
                def face(row0):
                    return at(FX, a if d > 0 else a - 1, row0)

                def e_at(row0):
                    return B1 * (at(INV, a, row0) * (face(row0) * at(y0, a + d, row0)))

                e, e_up, e_down = e_at(r0), e_at(r0 + 1), e_at(r0 - 1)
                fz, inv = at(FZ, a, r0), at(INV, a, r0)
                flow = face(r0) * at(y1, a + d, r0) + (
                    fz * pltpu.roll(e, nz - 1, 1) + pltpu.roll(fz * e, 1, 1)
                )
                side = at(FY, a, r0) * (pair_up * e_up) + at(FY, a, r0 - 1) * (pair_down * e_down)
                fix = times * (A2 * e + B2 * (inv * flow)) + B2 * (inv * side)
                put(z, a, r0, at(z, a, r0) - weight * fix)
                inner = at(FX, a - 1 if d > 0 else a, r0)
                fix = (weight * B2) * (times * (at(INV, a - d, r0) * (inner * e)))
                put(z, a - d, r0, at(z, a - d, r0) - fix)
            return carry

        strips(cut_edges)

        def over_x(x):
            if -MARGIN <= x < MARGIN:
                return m_lo
            if cx - MARGIN <= x < cx + MARGIN:
                return m_hi
            return 0.0

        def up(v):
            return pltpu.roll(v, 7, 0)

        def down(v):
            return pltpu.roll(v, 1, 0)

        sides = [(YO, 1, n_lo), (YO + cy - 8, -1, n_hi)]
        if reach == MARGIN:
            sides += [(YO - 8, -1, one), (YO + cy, 1, one)]
        for r0, d, weight in sides:
            edge = sub == (3 if d > 0 else 4)
            inner = sub == (2 if d > 0 else 5)

            def cross(fy, v):
                return fy * up(v) if d > 0 else down(fy * v)

            def e_of(x):
                return jnp.where(edge, B1 * (at(INV, x, r0, 8) * cross(at(FY, x, r0, 8), at(y0, x, r0, 8))), 0.0)

            prev, cur, f_prev = e_of(-reach - 1), e_of(-reach), at(FX, -reach - 1, r0, 8)
            for x in range(-reach, cx + reach):
                nxt, f = e_of(x + 1), at(FX, x, r0, 8)
                fy, fz, inv = at(FY, x, r0, 8), at(FZ, x, r0, 8), at(INV, x, r0, 8)
                times = 1.0 + over_x(x)
                flow = jnp.where(edge, cross(fy, at(y1, x, r0, 8)), 0.0)
                flow = flow + jnp.where(inner, cross(fy, cur), 0.0)
                flow = flow + (fz * pltpu.roll(cur, nz - 1, 1) + pltpu.roll(fz * cur, 1, 1))
                side = (1.0 + over_x(x) * over_x(x + 1)) * (f * nxt) if x + 1 != MARGIN and x + 1 != cx - MARGIN else f * nxt
                side = side + (
                    (1.0 + over_x(x) * over_x(x - 1)) * (f_prev * prev)
                    if x != MARGIN and x != cx - MARGIN else f_prev * prev
                )
                fix = times * (A2 * cur + B2 * (inv * flow)) + B2 * (inv * side)
                put(z, x, r0, at(z, x, r0, 8) - weight * fix)
                prev, cur, f_prev = cur, nxt, f

    zero = jnp.zeros((8, nz), jnp.float32)
    cut(Y0, Y1, Z0, MARGIN)

    def image0(r0, carry):
        def use(x, value, total):
            half = 0.5 * total
            put(Y0B, x, r0, (value - at(INV, x, r0) * half) * (1.0 / theta))
            if 0 <= x < cx:
                put(W0, x - XO, r0 - (YO - 8), at(DIAG, x, r0) * value - half)

        sweep(Z0, -3, cx + 3, r0, use)
        return carry

    strips(image0)
    precondition(Y0B, Y1, Z1, 1)

    def image1(t, carry):
        r0 = pl.multiple_of(YO + own_strip * t, 8)
        sums = list(carry)

        def use(x, value, total):
            w1 = at(DIAG, x, r0, own_strip) * value - 0.5 * total
            put(W1, x - XO, r0 - YO, w1)
            r, z0 = at(R, x, r0, own_strip), at(Z0, x, r0, own_strip)
            w0 = at(W0, x - XO, r0 - (YO - 8), own_strip)
            for q, (a, b) in enumerate(((r, z0), (z0, w0), (r, value), (w0, value), (z0, w1), (value, w1))):
                sums[q] = sums[q] + jnp.sum((a * b).reshape(own_strip // 8, 8, nz), axis=0)

        sweep(Z1, 0, cx, r0, use, own_strip)
        return tuple(sums)

    sums = lax.fori_loop(0, brick // own_strip, image1, (zero,) * 6)

    group_of = lax.broadcasted_iota(jnp.int32, (8, nz), 1) // 16
    mine = zero
    for q, acc in enumerate(sums):
        mine = jnp.where(sub == q, jnp.sum(acc, axis=0, keepdims=True), mine)
    for shift in (64, 32, 16):
        mine = mine + pltpu.roll(mine, shift, 1)
    part[0] = jnp.sum(jnp.where(sub == group_of, mine, 0.0), axis=0, keepdims=True)
    base = 0
    sent = []
    for s, dims in enumerate(STAGES):
        offs = offsets(dims)
        for n, off in enumerate(offs):
            pltpu.make_async_remote_copy(
                part.at[s], slots.at[base + n], ar_send.at[s], ar_recv.at[s],
                device_id=partner(gx, gy, dims, off), device_id_type=MESH,
            ).start()
        group = slots.at[pl.ds(base, len(offs))]
        both = pltpu.make_async_remote_copy(
            group, group, ar_send.at[s], ar_recv.at[s],
            device_id=partner(gx, gy, dims, offs[0]), device_id_type=MESH,
        )
        both.wait_recv()
        sent.append(both)
        part[s + 1] = part[s] + jnp.sum(slots[base : base + len(offs)], axis=0)
        base += len(offs)
    totals = jnp.where(sub == group_of, jnp.broadcast_to(part[len(STAGES)], (8, nz)), 0.0)
    totals = jnp.sum(totals, axis=1, keepdims=True)
    rz, zw, rz1, wz1, zw1, z1w1 = [totals[q : q + 1] for q in range(6)]
    step0 = rz / zw
    next_rz = rz - step0 * (rz1 + zw) + step0 * step0 * wz1
    grow = 1.0 + next_rz / rz
    curve = grow * grow * zw - grow * step0 * (zw1 + wz1) + step0 * step0 * z1w1
    step1 = next_rz / curve
    g0, g1 = step0 + step1 * grow, step1 * step0
    g0 = jnp.broadcast_to(g0, (brick, nz))
    g1 = jnp.broadcast_to(g1, (brick, nz))

    def finish(x, carry):
        z0, z1 = at(Z0, x, YO, brick), at(Z1, x, YO, brick)
        w0, w1 = at(W0, x - XO, 8, brick), at(W1, x - XO, 0, brick)
        sol[x] = g0 * z0 - g1 * z1
        res[x] = at(R, x, YO, brick) - g0 * w0 + g1 * w1
        return carry

    lax.fori_loop(0, cx, finish, 0)
    for both in sent:
        both.wait_send()
    for k, (dx, dy) in enumerate(NEAR):

        @pl.when(here(dx, dy))
        def _():
            for copy in halo_copies(k, dx, dy):
                copy.wait_send()


def shards(right_side, conductivity):
    cx, cy, nz = right_side.shape
    ext = pltpu.VMEM((cx + 2 * KW, cy + 2 * YO, nz), jnp.float32)
    dma = pltpu.SemaphoreType.DMA
    hbm = pl.BlockSpec(memory_space=pltpu.MemorySpace.HBM)
    out = jax.ShapeDtypeStruct((cx, cy, nz), jnp.float32)
    right_side, conductivity = (
        pltpu.with_memory_space_constraint(v, pltpu.MemorySpace.HBM) for v in (right_side, conductivity)
    )
    return pl.pallas_call(
        kernel,
        out_shape=(out, out),
        in_specs=[hbm, hbm],
        out_specs=(pl.BlockSpec(memory_space=pltpu.MemorySpace.VMEM),) * 2,
        scratch_shapes=[ext] * 12
        + [
            pltpu.VMEM((cx, cy + 16, nz), jnp.float32),
            pltpu.VMEM((cx, cy, nz), jnp.float32),
            pltpu.VMEM((2, SIDE * cx + 8, nz), jnp.float32),
            pltpu.VMEM((2, SIDE * cx + 16, nz), jnp.float32),
            pltpu.VMEM((4, CORNER_ROWS + 8, nz), jnp.float32),
            pltpu.VMEM((4, CORNER_ROWS + 16, nz), jnp.float32),
            pltpu.VMEM((len(STAGES) + 1, 1, nz), jnp.float32),
            pltpu.VMEM((N_SLOTS, 1, nz), jnp.float32),
            dma((2, 4)), dma((16,)), dma((16,)), dma((len(STAGES),)), dma((len(STAGES),)),
        ],
        compiler_params=pltpu.CompilerParams(
            collective_id=0, has_side_effects=True, vmem_limit_bytes=40 << 20
        ),
    )(right_side, conductivity)


def solution(mesh):
    spec = P("gx", "gy", None)
    return jax.shard_map(
        shards, mesh=mesh, in_specs=(spec, spec), out_specs=(spec, spec), check_vma=False
    )
```

```python
import itertools

import jax
import jax.numpy as jnp
from jax import lax
from jax.experimental import pallas as pl
from jax.experimental.pallas import tpu as pltpu
from jax.sharding import PartitionSpec as P

MESH = pl.DeviceIdType.MESH
MARGIN = 4
absorb = 0.05
theta = 1.05
delta = 0.95

sig = theta / delta
rho0 = 1.0 / sig
rho1 = 1.0 / (2.0 * sig - rho0)
rho2 = 1.0 / (2.0 * sig - rho1)
c1, c2 = rho1 * rho0, 2.0 * rho1 / delta
c3, c4 = rho2 * rho1, 2.0 * rho2 / delta
A1 = 1.0 + c1 + c2 * (theta - 1.0)
B1 = 0.5 * c2
A2 = 1.0 + c3 - c4
A0 = c4 * theta - c3
B2 = 0.5 * c4

KW, RW = 7, 6
GUARD = 8
YO = 16
XO = KW

SIZES = dict(c=2, x=4, y=4, z=8)
STAGES = (("c",), ("x", "y"), ("z",))
CORNERS = ((-1, -1), (-1, 1), (1, -1), (1, 1))
NEAR = CORNERS + ((0, -1), (0, 1), (-1, 0), (1, 0))


def offsets(dims):
    def hops(off):
        return sum(min(o, SIZES[d] - o) for d, o in zip(dims, off))

    every = itertools.product(*[range(SIZES[d]) for d in dims])
    return sorted((off for off in every if any(off)), key=hops, reverse=True)


N_SLOTS = sum(len(offsets(dims)) for dims in STAGES)


def partner(gx, gy, dims, off):
    me = dict(c=gx % 2, x=(gx // 2) % 4, y=gy % 4, z=gx // 8 + 4 * (gy // 4))
    for d, o in zip(dims, off):
        me[d] = (me[d] + o) % SIZES[d]
    return ((me["z"] % 4) * 8 + me["x"] * 2 + me["c"], (me["z"] // 4) * 4 + me["y"])


def triangle(start, width):
    out = []
    for d in range(1, width):
        out.append((d, start, width - d))
        start += width - d
    return out


K_CORNER = triangle(0, KW)
R_CORNER = triangle(sum(n for _, _, n in K_CORNER), RW)
CORNER_ROWS = 40
SIDE = KW + RW


def kernel(
    r_hbm, k_hbm, sol, res,
    K, R, INV, DIAG, FX, FY, FZ, Y0, Y1, Y0B, Z0, Z1, W0, W1, side_out, side_in, corner_out, corner_in, part, slots,
    load_sem, send_sem, recv_sem, ar_send, ar_recv,
):
    cx, cy, nz = r_hbm.shape
    n_gx, n_gy = lax.axis_size("gx"), lax.axis_size("gy")
    gx, gy = lax.axis_index("gx"), lax.axis_index("gy")
    full, brick = cy + 16, cy
    strip = 48 if full % 48 == 0 else 8
    own_strip = 64 if brick % 64 == 0 else 8

    def here(dx, dy):
        return (gx + dx >= 0) & (gx + dx < n_gx) & (gy + dy >= 0) & (gy + dy < n_gy)

    piece = cx // 4
    loads = [
        pltpu.make_async_copy(
            src.at[pl.ds(x, piece)], dst.at[pl.ds(XO + x, piece), pl.ds(YO, cy)], load_sem.at[n, x // piece]
        )
        for n, (src, dst) in enumerate(((k_hbm, K), (r_hbm, R)))
        for x in range(0, cx, piece)
    ]
    for load in loads:
        load.start()

    barrier = pltpu.get_barrier_semaphore()
    count = 0
    for dx, dy in NEAR:
        count = count + here(dx, dy).astype(jnp.int32)

        @pl.when(here(dx, dy))
        def _():
            pl.semaphore_signal(barrier, inc=1, device_id=(gx + dx, gy + dy), device_id_type=MESH)

    for dims in STAGES:
        for off in offsets(dims):
            pl.semaphore_signal(
                barrier, inc=1, device_id=partner(gx, gy, dims, off), device_id_type=MESH
            )
            count = count + 1

    for load in loads:
        load.wait()

    def pack(x, carry):
        for s, (k_row, r_row) in enumerate(((YO, YO), (YO + cy - KW, YO + cy - RW))):
            side_out[s, pl.ds(SIDE * x, 8)] = K[x + XO, pl.ds(k_row, 8)]
            side_out[s, pl.ds(SIDE * x + KW, 8)] = R[x + XO, pl.ds(r_row, 8)]
        return carry

    lax.fori_loop(0, cx, pack, 0)
    for c, (dx, dy) in enumerate(CORNERS):
        for ref, parts in ((K, K_CORNER), (R, R_CORNER)):
            for d, start, n in parts:
                x = XO + (cx - d if dx > 0 else d - 1)
                corner_out[c, pl.ds(start, 8)] = ref[x, pl.ds(YO + cy - n if dy > 0 else YO, 8)]

    pl.semaphore_wait(barrier, count)

    def halo_copies(k, dx, dy):
        if dx and dy:
            pairs = [(corner_out.at[k, pl.ds(0, CORNER_ROWS)], corner_in.at[k, pl.ds(8, CORNER_ROWS)])]
        elif dy:
            s = (dy + 1) // 2
            pairs = [(side_out.at[s, pl.ds(0, SIDE * cx)], side_in.at[s, pl.ds(8, SIDE * cx)])]
        else:
            pairs = []
            for src, dst, width in ((k_hbm, K, KW), (r_hbm, R, RW)):
                sx = cx - width if dx > 0 else 0
                tx = XO - width if dx > 0 else XO + cx
                pairs.append((src.at[pl.ds(sx, width)], dst.at[pl.ds(tx, width), pl.ds(YO, cy)]))
        return [
            pltpu.make_async_remote_copy(
                src, dst, send_sem.at[2 * k + n], recv_sem.at[2 * k + n],
                device_id=(gx + dx, gy + dy), device_id_type=MESH,
            )
            for n, (src, dst) in enumerate(pairs)
        ]

    def send(along_x, which):
        for k, (dx, dy) in enumerate(NEAR):
            if along_x == (dy == 0):

                @pl.when(here(dx, dy))
                def _():
                    halo_copies(k, dx, dy)[which].start()

    send(False, 0)
    send(True, 0)
    send(True, 1)

    sub = lax.broadcasted_iota(jnp.int32, (8, nz), 0)

    def line_of(h):
        return lax.broadcasted_iota(jnp.int32, (h, nz), 0)

    one = jnp.float32(1.0)
    m_lo = jnp.where(gx > 0, one, 0.0)
    m_hi = jnp.where(gx < n_gx - 1, one, 0.0)
    has_lo, has_hi = gy > 0, gy < n_gy - 1
    n_lo = jnp.where(has_lo, one, 0.0)
    n_hi = jnp.where(has_hi, one, 0.0)

    def at(ref, x, row, h=strip):
        return ref[x + XO, pl.ds(row, h), :]

    def put(ref, x, row, value):
        ref[x + XO, pl.ds(row, value.shape[0]), :] = value

    def strip_row(t):
        return pl.multiple_of(YO - 8 + strip * t, 8)

    def strips(body):
        lax.fori_loop(0, full // strip, lambda t, c: body(strip_row(t), c), 0)

    tall = 64 if cy % 64 == 0 else 8

    def inside(stage, m):
        def body(t, carry):
            stage(pl.multiple_of(YO + tall * t, 8), m, cx - m, tall)
            return carry

        lax.fori_loop(0, cy // tall, body, 0)

    def ends(stage, m):
        def body(t, carry):
            stage(pl.multiple_of(YO - 8 + cy * t, 8), m, cx - m, 16)
            return carry

        lax.fori_loop(0, 2, body, 0)

    def sides(stage, m, reach):
        def body(r0, carry):
            stage(r0, -reach, m, strip)
            stage(r0, cx - m, cx + reach, strip)
            return carry

        strips(body)

    def coefficients(r0, lo, hi, h):
        lane = lax.broadcasted_iota(jnp.int32, (h, nz), 1)
        first_lane, last_lane = lane == 0, lane == nz - 1
        low, mid = at(K, lo - 1, r0, h), at(K, lo, r0, h)
        for x in range(lo, hi):
            high = at(K, x + 1, r0, h)
            up, down = at(K, x, r0 + 1, h), at(K, x, r0 - 1, h)
            right = jnp.where(last_lane, mid, pltpu.roll(mid, nz - 1, 1))
            left = jnp.where(first_lane, mid, pltpu.roll(mid, 1, 1))
            diag = (absorb + 3.0 * mid) + 0.5 * ((low + high) + (up + down) + (left + right))
            inv = 1.0 / diag
            if 0 <= x < cx:
                put(DIAG, x, r0, diag)
            put(INV, x, r0, inv)
            put(FX, x, r0, mid + high)
            put(FY, x, r0, mid + up)
            put(FZ, x, r0, jnp.where(last_lane, 0.0, mid + right))
            low, mid = mid, high

    def start(r0, lo, hi, h):
        for x in range(lo, hi):
            put(Y0, x, r0, at(R, x, r0, h) * (at(INV, x, r0, h) * (1.0 / theta)))

    def sweep(src, lo, hi, r0, use, h=strip):
        prev, cur, f_prev = at(src, lo - 1, r0, h), at(src, lo, r0, h), at(FX, lo - 1, r0, h)
        for x in range(lo, hi):
            nxt, f = at(src, x + 1, r0, h), at(FX, x, r0, h)
            fz = at(FZ, x, r0, h)
            total = f * nxt + f_prev * prev
            total = total + (
                at(FY, x, r0, h) * at(src, x, r0 + 1, h) + at(FY, x, r0 - 1, h) * at(src, x, r0 - 1, h)
            )
            total = total + (fz * pltpu.roll(cur, nz - 1, 1) + pltpu.roll(fz * cur, 1, 1))
            use(x, cur, total)
            prev, cur, f_prev = cur, nxt, f

    def in_overlap(row):
        return ((row >= -MARGIN) & (row < MARGIN) & has_lo) | (
            (row >= cy - MARGIN) & (row < cy + MARGIN) & has_hi
        )

    def counts(r0, h):
        row = line_of(h) + (r0 - YO)
        over = jnp.where(in_overlap(row), one, 0.0)
        return row, over, 1.0 + over

    def first(y0, y1):
        def stage(r0, lo, hi, h):
            def use(x, value, total):
                put(y1, x, r0, A1 * value + B1 * (at(INV, x, r0, h) * total))

            sweep(y0, lo, hi, r0, use, h)

        return stage

    def second(y0, y1, z):
        def stage(r0, lo, hi, h):
            _, _, times = counts(r0, h)

            def use(x, value, total):
                y2 = A2 * value + A0 * at(y0, x, r0, h) + B2 * (at(INV, x, r0, h) * total)
                weight = 1.0 + m_lo if x < MARGIN else (1.0 + m_hi if x >= cx - MARGIN else one)
                put(z, x, r0, (weight * times) * y2)

            sweep(y1, lo, hi, r0, use, h)

        return stage

    inside(coefficients, 1)
    inside(start, 1)
    inside(first(Y0, Y1), 2)
    inside(second(Y0, Y1, Z0), 3)

    rows = cy + 16
    flat = lambda n: jnp.zeros((n, nz), jnp.float32)

    @pl.when(gx == 0)
    def _():
        for x in range(XO):
            K[x, pl.ds(YO - 8, rows)] = flat(rows)
            R[x, pl.ds(YO - 8, rows)] = flat(rows)

    @pl.when(gx == n_gx - 1)
    def _():
        for x in range(XO + cx, XO + cx + KW):
            K[x, pl.ds(YO - 8, rows)] = flat(rows)
            R[x, pl.ds(YO - 8, rows)] = flat(rows)


    def receive(along_x, which):
        for k, (dx, dy) in enumerate(NEAR):
            if along_x == (dy == 0):

                @pl.when(here(-dx, -dy))
                def _():
                    halo_copies(k, dx, dy)[which].wait_recv()

    receive(False, 0)

    for s, (dy, k_off, r_off) in enumerate(((-1, 8, 8 + KW), (1, 8 + KW - 8, 8 + SIDE - 8))):

        @pl.when(here(0, -dy))
        def _():
            row = YO - 8 if dy > 0 else YO + cy

            def unpack(x, carry):
                K[x + XO, pl.ds(row, 8)] = side_in[s, pl.ds(SIDE * x + k_off, 8)]
                R[x + XO, pl.ds(row, 8)] = side_in[s, pl.ds(SIDE * x + r_off, 8)]
                return carry

            lax.fori_loop(0, cx, unpack, 0)

    for c, (dx, dy) in enumerate(CORNERS):

        @pl.when(here(-dx, -dy))
        def _():
            row = YO - 8 if dy > 0 else YO + cy
            for ref, parts in ((K, K_CORNER), (R, R_CORNER)):
                for d, start, n in parts:
                    x = XO + (-d if dx > 0 else cx + d - 1)
                    ref[x, pl.ds(row, 8)] = corner_in[c, pl.ds(start + (n if dy > 0 else 8), 8)]

    own_layers = tuple(range(XO, XO + cx))
    halo_layers = tuple(range(XO)) + tuple(range(XO + cx, cx + 2 * KW))

    def mirror(layers):
        @pl.when(gy == 0)
        def _():
            for x in layers:
                K[x, pl.ds(YO - 8, 8)] = jnp.broadcast_to(K[x, pl.ds(YO, 1)], (8, nz))
                R[x, pl.ds(YO - 8, 8)] = flat(8)

        @pl.when(gy == n_gy - 1)
        def _():
            for x in layers:
                K[x, pl.ds(YO + cy, 8)] = jnp.broadcast_to(K[x, pl.ds(YO + cy - 1, 1)], (8, nz))
                R[x, pl.ds(YO + cy, 8)] = flat(8)

    def cut_faces(layers):
        @pl.when(gy == 0)
        def _():
            for x in layers:
                FY[x, pl.ds(YO - 1, 1)] = flat(1)

        @pl.when(gy == n_gy - 1)
        def _():
            for x in layers:
                FY[x, pl.ds(YO + cy - 1, 1)] = flat(1)

    mirror(own_layers)
    ends(coefficients, 1)
    ends(start, 1)
    cut_faces(own_layers)
    ends(first(Y0, Y1), 2)
    ends(second(Y0, Y1, Z0), 3)

    def take(dx, which):
        k = NEAR.index((dx, 0))

        @pl.when(here(-dx, 0))
        def _():
            halo_copies(k, dx, 0)[which].wait_recv()

    def side_of(dx):
        halo = tuple(range(XO)) if dx > 0 else tuple(range(XO + cx, cx + 2 * KW))
        edge, outer = (XO, XO - 1) if dx > 0 else (XO + cx - 1, XO + cx)
        at_end = gx == 0 if dx > 0 else gx == n_gx - 1

        def run(stage, m, reach):
            def body(r0, carry):
                if dx > 0:
                    stage(r0, -reach, m, strip)
                else:
                    stage(r0, cx - m, cx + reach, strip)
                return carry

            strips(body)

        take(dx, 0)

        @pl.when(at_end)
        def _():
            K[outer, pl.ds(YO - 8, rows)] = K[edge, pl.ds(YO - 8, rows)]

        mirror(halo)
        run(coefficients, 1, RW)
        take(dx, 1)
        run(start, 1, RW)

        @pl.when(at_end)
        def _():
            FX[min(edge, outer), pl.ds(YO - 8, rows)] = flat(rows)

        cut_faces(halo + (edge,))
        run(first(Y0, Y1), 2, MARGIN + 1)
        run(second(Y0, Y1, Z0), 3, MARGIN)

    even = gx % 2 == 0
    for turn in (True, False):
        for dx in (-1, 1):

            @pl.when(even == (turn == (dx < 0)))
            def _():
                side_of(dx)

    def precondition(y0, y1, z, reach):
        strips(lambda r0, c: (first(y0, y1)(r0, -reach - 1, cx + reach + 1, strip), c)[1])
        strips(lambda r0, c: (second(y0, y1, z)(r0, -reach, cx + reach, strip), c)[1])
        cut(y0, y1, z, reach)

    def cut(y0, y1, z, reach):
        edges = [(MARGIN - 1, 1, m_lo), (cx - MARGIN, -1, m_hi)]
        if reach == MARGIN:
            edges += [(-MARGIN, -1, one), (cx + MARGIN - 1, 1, one)]

        def cut_edges(r0, carry):
            row, over, times = counts(r0, strip)
            pair_up = 1.0 + over * jnp.where(in_overlap(row + 1), one, 0.0)
            pair_down = 1.0 + over * jnp.where(in_overlap(row - 1), one, 0.0)
            for a, d, weight in edges:
                def face(row0):
                    return at(FX, a if d > 0 else a - 1, row0)

                def e_at(row0):
                    return B1 * (at(INV, a, row0) * (face(row0) * at(y0, a + d, row0)))

                e, e_up, e_down = e_at(r0), e_at(r0 + 1), e_at(r0 - 1)
                fz, inv = at(FZ, a, r0), at(INV, a, r0)
                flow = face(r0) * at(y1, a + d, r0) + (
                    fz * pltpu.roll(e, nz - 1, 1) + pltpu.roll(fz * e, 1, 1)
                )
                side = at(FY, a, r0) * (pair_up * e_up) + at(FY, a, r0 - 1) * (pair_down * e_down)
                fix = times * (A2 * e + B2 * (inv * flow)) + B2 * (inv * side)
                put(z, a, r0, at(z, a, r0) - weight * fix)
                inner = at(FX, a - 1 if d > 0 else a, r0)
                fix = (weight * B2) * (times * (at(INV, a - d, r0) * (inner * e)))
                put(z, a - d, r0, at(z, a - d, r0) - fix)
            return carry

        strips(cut_edges)

        def over_x(x):
            if -MARGIN <= x < MARGIN:
                return m_lo
            if cx - MARGIN <= x < cx + MARGIN:
                return m_hi
            return 0.0

        def up(v):
            return pltpu.roll(v, 7, 0)

        def down(v):
            return pltpu.roll(v, 1, 0)

        sides = [(YO, 1, n_lo), (YO + cy - 8, -1, n_hi)]
        if reach == MARGIN:
            sides += [(YO - 8, -1, one), (YO + cy, 1, one)]
        for r0, d, weight in sides:
            edge = sub == (3 if d > 0 else 4)
            inner = sub == (2 if d > 0 else 5)

            def cross(fy, v):
                return fy * up(v) if d > 0 else down(fy * v)

            def e_of(x):
                return jnp.where(edge, B1 * (at(INV, x, r0, 8) * cross(at(FY, x, r0, 8), at(y0, x, r0, 8))), 0.0)

            prev, cur, f_prev = e_of(-reach - 1), e_of(-reach), at(FX, -reach - 1, r0, 8)
            for x in range(-reach, cx + reach):
                nxt, f = e_of(x + 1), at(FX, x, r0, 8)
                fy, fz, inv = at(FY, x, r0, 8), at(FZ, x, r0, 8), at(INV, x, r0, 8)
                times = 1.0 + over_x(x)
                flow = jnp.where(edge, cross(fy, at(y1, x, r0, 8)), 0.0)
                flow = flow + jnp.where(inner, cross(fy, cur), 0.0)
                flow = flow + (fz * pltpu.roll(cur, nz - 1, 1) + pltpu.roll(fz * cur, 1, 1))
                side = (1.0 + over_x(x) * over_x(x + 1)) * (f * nxt) if x + 1 != MARGIN and x + 1 != cx - MARGIN else f * nxt
                side = side + (
                    (1.0 + over_x(x) * over_x(x - 1)) * (f_prev * prev)
                    if x != MARGIN and x != cx - MARGIN else f_prev * prev
                )
                fix = times * (A2 * cur + B2 * (inv * flow)) + B2 * (inv * side)
                put(z, x, r0, at(z, x, r0, 8) - weight * fix)
                prev, cur, f_prev = cur, nxt, f

    zero = jnp.zeros((8, nz), jnp.float32)
    cut(Y0, Y1, Z0, MARGIN)

    def image0(r0, carry):
        def use(x, value, total):
            half = 0.5 * total
            put(Y0B, x, r0, (value - at(INV, x, r0) * half) * (1.0 / theta))
            if 0 <= x < cx:
                put(W0, x - XO, r0 - (YO - 8), at(DIAG, x, r0) * value - half)

        sweep(Z0, -3, cx + 3, r0, use)
        return carry

    strips(image0)
    precondition(Y0B, Y1, Z1, 1)

    def image1(t, carry):
        r0 = pl.multiple_of(YO + own_strip * t, 8)
        sums = list(carry)

        def use(x, value, total):
            w1 = at(DIAG, x, r0, own_strip) * value - 0.5 * total
            put(W1, x - XO, r0 - YO, w1)
            r, z0 = at(R, x, r0, own_strip), at(Z0, x, r0, own_strip)
            w0 = at(W0, x - XO, r0 - (YO - 8), own_strip)
            for q, (a, b) in enumerate(((r, z0), (z0, w0), (r, value), (w0, value), (z0, w1), (value, w1))):
                sums[q] = sums[q] + jnp.sum((a * b).reshape(own_strip // 8, 8, nz), axis=0)

        sweep(Z1, 0, cx, r0, use, own_strip)
        return tuple(sums)

    sums = lax.fori_loop(0, brick // own_strip, image1, (zero,) * 6)

    group_of = lax.broadcasted_iota(jnp.int32, (8, nz), 1) // 16
    mine = zero
    for q, acc in enumerate(sums):
        mine = jnp.where(sub == q, jnp.sum(acc, axis=0, keepdims=True), mine)
    for shift in (64, 32, 16):
        mine = mine + pltpu.roll(mine, shift, 1)
    part[0] = jnp.sum(jnp.where(sub == group_of, mine, 0.0), axis=0, keepdims=True)
    base = 0
    sent = []
    for s, dims in enumerate(STAGES):
        offs = offsets(dims)
        for n, off in enumerate(offs):
            pltpu.make_async_remote_copy(
                part.at[s], slots.at[base + n], ar_send.at[s], ar_recv.at[s],
                device_id=partner(gx, gy, dims, off), device_id_type=MESH,
            ).start()
        group = slots.at[pl.ds(base, len(offs))]
        both = pltpu.make_async_remote_copy(
            group, group, ar_send.at[s], ar_recv.at[s],
            device_id=partner(gx, gy, dims, offs[0]), device_id_type=MESH,
        )
        both.wait_recv()
        sent.append(both)
        part[s + 1] = part[s] + jnp.sum(slots[base : base + len(offs)], axis=0)
        base += len(offs)
    totals = jnp.where(sub == group_of, jnp.broadcast_to(part[len(STAGES)], (8, nz)), 0.0)
    totals = jnp.sum(totals, axis=1, keepdims=True)
    rz, zw, rz1, wz1, zw1, z1w1 = [totals[q : q + 1] for q in range(6)]
    step0 = rz / zw
    next_rz = rz - step0 * (rz1 + zw) + step0 * step0 * wz1
    grow = 1.0 + next_rz / rz
    curve = grow * grow * zw - grow * step0 * (zw1 + wz1) + step0 * step0 * z1w1
    step1 = next_rz / curve
    g0, g1 = step0 + step1 * grow, step1 * step0
    g0 = jnp.broadcast_to(g0, (brick, nz))
    g1 = jnp.broadcast_to(g1, (brick, nz))

    def finish(x, carry):
        z0, z1 = at(Z0, x, YO, brick), at(Z1, x, YO, brick)
        w0, w1 = at(W0, x - XO, 8, brick), at(W1, x - XO, 0, brick)
        sol[x] = g0 * z0 - g1 * z1
        res[x] = at(R, x, YO, brick) - g0 * w0 + g1 * w1
        return carry

    lax.fori_loop(0, cx, finish, 0)
    for both in sent:
        both.wait_send()
    for k, (dx, dy) in enumerate(NEAR):

        @pl.when(here(dx, dy))
        def _():
            for copy in halo_copies(k, dx, dy):
                copy.wait_send()


def shards(right_side, conductivity):
    cx, cy, nz = right_side.shape
    ext = pltpu.VMEM((cx + 2 * KW, cy + 2 * YO, nz), jnp.float32)
    dma = pltpu.SemaphoreType.DMA
    hbm = pl.BlockSpec(memory_space=pltpu.MemorySpace.HBM)
    out = jax.ShapeDtypeStruct((cx, cy, nz), jnp.float32)
    right_side, conductivity = (
        pltpu.with_memory_space_constraint(v, pltpu.MemorySpace.HBM) for v in (right_side, conductivity)
    )
    return pl.pallas_call(
        kernel,
        out_shape=(out, out),
        in_specs=[hbm, hbm],
        out_specs=(pl.BlockSpec(memory_space=pltpu.MemorySpace.VMEM),) * 2,
        scratch_shapes=[ext] * 12
        + [
            pltpu.VMEM((cx, cy + 16, nz), jnp.float32),
            pltpu.VMEM((cx, cy, nz), jnp.float32),
            pltpu.VMEM((2, SIDE * cx + 8, nz), jnp.float32),
            pltpu.VMEM((2, SIDE * cx + 16, nz), jnp.float32),
            pltpu.VMEM((4, CORNER_ROWS + 8, nz), jnp.float32),
            pltpu.VMEM((4, CORNER_ROWS + 16, nz), jnp.float32),
            pltpu.VMEM((len(STAGES) + 1, 1, nz), jnp.float32),
            pltpu.VMEM((N_SLOTS, 1, nz), jnp.float32),
            dma((2, 4)), dma((16,)), dma((16,)), dma((len(STAGES),)), dma((len(STAGES),)),
        ],
        compiler_params=pltpu.CompilerParams(
            collective_id=0, has_side_effects=True, vmem_limit_bytes=40 << 20
        ),
    )(right_side, conductivity)


def solution(mesh):
    spec = P("gx", "gy", None)
    return jax.shard_map(
        shards, mesh=mesh, in_specs=(spec, spec), out_specs=(spec, spec), check_vma=False
    )
```
